128 devices in a mesh: expert: 32 (over z, x, core), etp: 4 (over y).
Axes of the slice: x: 4, y: 4, z: 4, core: 2. Of those that a mesh axis runs over, the one named last changes fastest.
Arguments:
- tokens: bfloat16 [16384, 2560], P(('expert', 'etp')), may hold values from -6 to 6
- routes: int32 [16384, 1], P(('expert', 'etp')), may hold values from 0 to 31; in each aligned block of 128 rows (0 to 127, 128 to 255, ...) at most 12 rows name the same one
- scores: float32 [16384], P(('expert', 'etp')), may hold values from 0.1 to 1
- gate_weight: bfloat16 [32, 2560, 4096], P('expert', None, 'etp'), may hold values from -0.125 to 0.125
- up_weight: bfloat16 [32, 2560, 4096], P('expert', None, 'etp'), may hold values from -0.125 to 0.125
- down_weight: bfloat16 [32, 4096, 2560], P('expert', 'etp'), may hold values from -0.09375 to 0.09375
Outputs:
- layer_out: bfloat16 [16384, 2560], P(('expert', 'etp'))
The draws below stay inside these ranges and needn't reach their ends.
Inputs may be any that keep to these rules, and one draw needn't show every extreme that they name: `routes`: within each device's aligned block of 128 rows no expert is named by more than 12 rows, a bound that some block reaches; every expert is named by some row.
All inputs are finite; a program needn't handle non-finite values.
Results may differ from the reference program's by a relative error of at most 0.014.
Values may be sent and summed in bfloat16 or wider, within the bound.
A program may use at most 128 MiB of HBM per device.

```python
import math
import jax
import jax.numpy as jnp
import numpy as np
from jax import lax

D = 2560
H = 4096
TOK_DEV = 128
EXPERTS = 32
CAP = 12
TOKENS = 16384
N_ETP = 4


def level_of(rng, extent, split, low, largest):
    def one(axis_at, parts):
        heights = jax.random.uniform(jax.random.fold_in(jax.random.fold_in(rng, 6), axis_at), (parts,), jnp.float32, low / len(split), largest / len(split))
        return jnp.repeat(jnp.exp(heights), extent[axis_at] // parts).reshape((-1,) + (1,) * (len(extent) - axis_at - 1))

    level = one(*split[0])
    for cut in split[1:]:
        level = level * one(*cut)
    return level


def routed_block(own_key, own, number, rows, amount, top, most, slope):
    ranking = jax.random.permutation(own_key, amount)
    heavy_load, usual = portions_of(amount, rows * top, most, slope, True), portions_of(amount, rows * top, most, slope, False)
    places = jnp.arange(amount)

    def named(sizes, rotation):
        used = int((sizes > 0).sum())
        fixed = max(1, used // 4)
        moved = fixed + (places - fixed + rotation * (used - fixed)) % max(1, amount - fixed)
        return jnp.zeros((amount,), jnp.int32).at[ranking[jnp.where(places < fixed, places, moved)]].set(jnp.asarray(sizes, jnp.int32))

    sizes = jnp.where(number % 4 == 0, named(heavy_load, number // 4), named(usual, number - number // 4 - 1))
    mixed = jax.random.permutation(jax.random.fold_in(own, 3), amount)
    source_of, receiver = mixed[0:amount // 2 * 2:2], mixed[1:amount // 2 * 2:2]
    slack = jnp.minimum(sizes[source_of] - 1, most - sizes[receiver]) // 2
    slack = jnp.where((source_of == ranking[0]) | (receiver == ranking[0]) | (sizes[receiver] == 0), 0, jnp.maximum(slack, 0))
    moved = jax.random.randint(jax.random.fold_in(own, 4), (amount // 2,), 0, 1 << 20) % (slack + 1)
    sizes = sizes.at[source_of].add(-moved).at[receiver].add(moved)
    items = jnp.searchsorted(jnp.cumsum(sizes), jnp.arange(rows * top), side="right").astype(jnp.int32)
    listing = items.reshape(top, rows).T
    listing = listing[jax.random.permutation(jax.random.fold_in(own, 1), rows)]
    rotation = jax.random.randint(jax.random.fold_in(own, 2), (rows, 1), 0, top)
    return jnp.take_along_axis(listing, (jnp.arange(top)[None, :] + rotation) % top, axis=1)


def portions_of(count, total, bound, lean, full):
    portions = [(1 << 20) // math.isqrt(rank ** lean) + 1 for rank in range(1, count + 1)]
    largest = bound if full else min(bound, max(-(-total // count), total * portions[0] // sum(portions)))
    least = 1 if total - largest >= count - 1 else 0
    holding, spare = [largest] + [least] * (count - 1), total - largest - least * (count - 1)
    while spare > 0:
        movable = [i for i in range(1, count) if holding[i] < largest] or [i for i in range(1, count) if holding[i] < bound]
        whole, remaining = sum([portions[i] for i in movable]), spare
        for i in movable:
            addition = min(bound - holding[i], max(1, remaining * portions[i] // whole), spare)
            holding[i] = holding[i] + addition
            spare = spare - addition
    return np.array(holding)


def normal_values(rng, dims, spread, most, cuts=(), kind=jnp.bfloat16):
    array = jax.random.normal(rng, dims, jnp.float32) * spread
    if len(cuts) > 0:
        array = level_of(rng, dims, cuts, -0.22, 0.18) * array
    return jnp.clip(array, min=-most, max=most).astype(kind)


def setup_inputs(seed: int = 0) -> dict:
    key_list = jax.random.split(jax.random.key(seed), 7)
    tokens = normal_values(key_list[0], (TOKENS, D), 1.0, 6.0, ((0, 128),))
    routes_keys = jax.random.split(jax.random.fold_in(key_list[1], 1), TOKENS // TOK_DEV)
    routes_turns = jax.random.permutation(jax.random.fold_in(key_list[1], 3), TOKENS // TOK_DEV)
    routes = jax.vmap(lambda own, number: routed_block(jax.random.fold_in(key_list[1], 2), own, number, TOK_DEV, EXPERTS, 1, CAP, 2))(routes_keys, routes_turns).reshape((TOKENS, 1))
    scores = jnp.clip(jnp.exp(math.log(1.0) - 2.3025851 * jax.random.uniform(key_list[2], (TOKENS,), jnp.float32) ** level_of(key_list[2], (TOKENS,), ((0, 128),), -0.2, 0.2)), 0.1, 1.0)
    gate_weight = normal_values(key_list[3], (EXPERTS, D, H), D ** -0.5, 0.125, ((0, 32), (2, 4)))
    up_weight = normal_values(key_list[4], (EXPERTS, D, H), D ** -0.5, 0.125, ((0, 32), (2, 4)))
    down_weight = normal_values(key_list[5], (EXPERTS, H, D), H ** -0.5, 0.09375, ((0, 32), (1, 4)))
    return dict(tokens=tokens, routes=routes, scores=scores, gate_weight=gate_weight, up_weight=up_weight, down_weight=down_weight)


def reference(tokens, routes, scores, gate_weight, up_weight, down_weight):
    block_rows = 128
    block_count = TOKENS // block_rows + EXPERTS
    expert_ids = routes[:, 0].astype(jnp.int32)
    onehot = (expert_ids[:, None] == jnp.arange(EXPERTS, dtype=jnp.int32)[None, :]).astype(jnp.int32)
    per_expert = jnp.sum(onehot, axis=0, dtype=jnp.int32)
    position = jnp.sum((jnp.cumsum(onehot, axis=0, dtype=jnp.int32) - 1) * onehot, axis=1, dtype=jnp.int32)
    padded = (per_expert + block_rows - 1) // block_rows * block_rows
    block_ends = jnp.cumsum(padded, dtype=jnp.int32)
    block_starts = block_ends - padded
    location = (jnp.sum(onehot * block_starts[None, :], axis=1, dtype=jnp.int32) + position).astype(jnp.int32)
    sectioning = jnp.zeros((block_count * block_rows, D), jnp.bfloat16).at[location].set(tokens)
    marks = (jnp.arange(block_count, dtype=jnp.int32) * block_rows).astype(jnp.int32)
    owners = jnp.sum((block_ends[None, :] <= marks[:, None]).astype(jnp.int32), axis=1, dtype=jnp.int32)
    owners = jnp.minimum(owners, EXPERTS - 1).astype(jnp.int32)
    row_blocks = sectioning.reshape(block_count, block_rows, D)
    quarter = H // N_ETP

    def compute(element):
        row_block, expert_id = element
        gate_out = jnp.dot(row_block, gate_weight[expert_id], preferred_element_type=jnp.float32)
        up_out = jnp.dot(row_block, up_weight[expert_id], preferred_element_type=jnp.float32)
        hidden = (jax.nn.silu(gate_out) * up_out).astype(jnp.bfloat16)
        down_local = down_weight[expert_id]
        summed = jnp.zeros((block_rows, D), jnp.float32)
        for partial_id in range(N_ETP):
            partial_value = jnp.dot(hidden[:, partial_id * quarter:(partial_id + 1) * quarter],
                              down_local[partial_id * quarter:(partial_id + 1) * quarter],
                              preferred_element_type=jnp.float32).astype(jnp.bfloat16)
            summed = summed + lax.optimization_barrier(partial_value).astype(jnp.float32)
        return summed.astype(jnp.bfloat16)

    results = lax.map(compute, (row_blocks, owners)).reshape(block_count * block_rows, D)
    expert_out = results[location]
    return (expert_out.astype(jnp.float32) * scores[:, None]).astype(jnp.bfloat16)
```

```python
import jax
import jax.numpy as jnp
from jax import lax
from jax.sharding import PartitionSpec as P


def hidden_rows(row_block, gate_local, up_local):
    flattened = row_block.reshape(-1, row_block.shape[-1])
    gate_out = jnp.dot(flattened, gate_local, preferred_element_type=jnp.float32)
    up_out = jnp.dot(flattened, up_local, preferred_element_type=jnp.float32)
    hidden = (jax.nn.silu(gate_out) * up_out).astype(jnp.bfloat16)
    return hidden.reshape(row_block.shape[:-1] + (gate_local.shape[1],))


def local(tokens, routes, scores, gate_weight, up_weight, down_weight):
    experts = lax.axis_size("expert")
    tok_rows, features = tokens.shape
    slot_count = 3 * tok_rows // experts
    expert_ids = routes[:, 0]
    earlier = jnp.arange(tok_rows)[:, None] < jnp.arange(tok_rows)[None, :]
    same = expert_ids[:, None] == expert_ids[None, :]
    position = jnp.sum((same & earlier).astype(jnp.int32), axis=0, dtype=jnp.int32)
    target = expert_ids * slot_count + position
    placing = (
        target[None, :] == jnp.arange(experts * slot_count, dtype=jnp.int32)[:, None]
    ).astype(jnp.bfloat16)
    outgoing = jnp.dot(placing, tokens, preferred_element_type=jnp.float32).astype(jnp.bfloat16)
    outgoing = outgoing.reshape(experts, slot_count, features)
    gate_local = gate_weight[0]
    up_local = up_weight[0]
    down_local = down_weight[0]
    received = lax.all_to_all(outgoing, "expert", split_axis=0, concat_axis=0, tiled=True)
    grouped = lax.all_gather(
        received.reshape(experts * slot_count, features), "etp", axis=0, tiled=True
    )
    hidden = hidden_rows(grouped, gate_local, up_local)
    partial_value = jnp.dot(hidden, down_local, preferred_element_type=jnp.float32)
    partial_value = partial_value.astype(jnp.bfloat16)
    summed = lax.psum_scatter(partial_value, "etp", scatter_dimension=0, tiled=True)
    summed = lax.all_to_all(
        summed.reshape(experts, slot_count, features),
        "expert",
        split_axis=0,
        concat_axis=0,
        tiled=True,
    )
    collected = lax.dot_general(
        placing,
        summed.reshape(experts * slot_count, features),
        (((0,), (0,)), ((), ())),
        preferred_element_type=jnp.float32,
    )
    return (collected * scores[:, None]).astype(jnp.bfloat16)


def solution(mesh):
    in_specs = (
        P(("expert", "etp"), None),
        P(("expert", "etp"), None),
        P(("expert", "etp")),
        P("expert", None, "etp"),
        P("expert", None, "etp"),
        P("expert", "etp", None),
    )
    out_specs = P(("expert", "etp"), None)
    return jax.shard_map(local, mesh=mesh, in_specs=in_specs, out_specs=out_specs, check_vma=False)
```

```python
import jax
import jax.numpy as jnp
from jax import lax
from jax.experimental import pallas as pl
from jax.experimental.pallas import tpu as pltpu
from jax.sharding import PartitionSpec as P

MESH = pl.DeviceIdType.MESH
CAP = 12
ORDER = (0, 1, 3, 2)


def layer(
    tokens,
    routes_row,
    routes_col,
    scores,
    gate_hbm,
    up_hbm,
    down_hbm,
    out,
    gate,
    up,
    down,
    codes,
    partner_codes,
    partner_tokens,
    place,
    outgoing,
    rows_in,
    lhs,
    hidden,
    partials,
    far,
    near,
    returned,
    cross_out,
    cross_in,
    weight_sem,
    pair_s,
    pair_r,
    zx_s,
    zx_r,
    hop1_s,
    hop1_r,
    hop2_s,
    hop2_r,
    far_s,
    far_r,
    near_s,
    near_r,
    back_s,
    back_r,
):
    e, y = lax.axis_index("expert"), lax.axis_index("etp")
    core, x, z = e % 2, (e // 2) % 4, e // 8
    features = tokens.shape[1]
    chunk_rows = lhs.shape[0]
    partner = (e + 1 - 2 * core, y)
    ups, downs = (e, (y + 1) % 4), (e, (y + 3) % 4)

    def owner(dz, dx):
        return ((((z + dz) % 4) * 4 + (x + dx) % 4) * 2 + core, y)

    def remote(src, dst, send, recv, to):
        return pltpu.make_async_remote_copy(
            src_ref=src, dst_ref=dst, send_sem=send, recv_sem=recv, device_id=to, device_id_type=MESH
        )

    weights = [
        pltpu.make_async_copy(gate_hbm, gate, weight_sem.at[0]),
        pltpu.make_async_copy(up_hbm, up, weight_sem.at[1]),
        pltpu.make_async_copy(down_hbm, down, weight_sem.at[2]),
    ]

    swap_tokens = remote(tokens, partner_tokens, pair_s.at[0], pair_r.at[0], partner)
    swap_tokens.start()
    for w in weights:
        w.start()
    tok = tokens.shape[0]
    row = routes_row[...]
    col = routes_col[...]
    first = lax.broadcasted_iota(jnp.int32, (tok, tok), 0)
    second = lax.broadcasted_iota(jnp.int32, (tok, tok), 1)
    same = col == row

    def code_of(route, position):
        chip = ((route // 8 - z) & 3) * 4 + ((route // 2 - x) & 3)
        return (route & 1) * 1024 + chip * (2 * CAP) + core * CAP + position

    pos_row = jnp.sum(jnp.where(same & (first < second), 1.0, 0.0), axis=0, keepdims=True)
    pos_col = jnp.sum(jnp.where(same & (second < first), 1.0, 0.0), axis=1, keepdims=True)
    codes[0:tok, :] = jnp.broadcast_to(code_of(col, pos_col.astype(jnp.int32)), (tok, tok))
    codes[tok : tok + 8, :] = jnp.broadcast_to(code_of(row, pos_row.astype(jnp.int32)), (8, tok))
    swap_codes = remote(codes, partner_codes, pair_s.at[1], pair_r.at[1], partner)
    swap_codes.start()
    slots = place.shape[0]
    slot = lax.broadcasted_iota(jnp.int32, (slots, tok), 0)

    def marks(code):
        return jnp.where(slot == code - core * 1024, 1.0, 0.0).astype(jnp.bfloat16)

    place[:, 0:tok] = marks(codes[tok : tok + 1, :])
    swap_codes.wait_recv()
    place[:, tok : 2 * tok] = marks(partner_codes[tok : tok + 1, :])
    swap_tokens.wait_recv()

    def send_zx(dz, dx):
        o = (4 - dz) % 4
        s = (4 - dx) % 4
        return remote(
            outgoing.at[dz, pl.ds(3 * dx, 3)],
            rows_in.at[o, 0, pl.ds(3 * s, 3)],
            zx_s.at[dz * 4 + dx],
            zx_r.at[o * 4 + s],
            owner(dz, dx),
        )

    def hop1(o, up_way, half):
        part = pl.ds(6 * half, 6)
        k = o * 4 + up_way * 2 + half
        return remote(
            rows_in.at[o, 0, part],
            rows_in.at[o, 3 if up_way else 1, part],
            hop1_s.at[k],
            hop1_r.at[k],
            ups if up_way else downs,
        )

    def hop2(o, up_way):
        part = pl.ds(0 if up_way else 6, 6)
        k = o * 2 + up_way
        return remote(
            rows_in.at[o, 3 if up_way else 1, part],
            rows_in.at[o, 2, part],
            hop2_s.at[k],
            hop2_r.at[k],
            ups if up_way else downs,
        )

    def send_far(o, up_way):
        k = o * 2 + up_way
        return remote(
            partials.at[o, 2, pl.ds(0 if up_way else 6, 6)],
            far.at[o, up_way],
            far_s.at[k],
            far_r.at[k],
            ups if up_way else downs,
        )

    def send_near(o, up_way, half):
        part = pl.ds(6 * half, 6)
        k = o * 4 + up_way * 2 + half
        return remote(
            partials.at[o, 1 if up_way else 3, part],
            near.at[o, up_way, part],
            near_s.at[k],
            near_r.at[k],
            ups if up_way else downs,
        )

    def send_back(o, dx):
        v, s = (4 - o) % 4, (4 - dx) % 4
        return remote(
            partials.at[o, 0, pl.ds(3 * dx, 3)],
            returned.at[v, pl.ds(3 * s, 3)],
            back_s.at[o * 4 + dx],
            back_r.at[v * 4 + s],
            owner(o, dx),
        )

    group = slots // 4
    for o in ORDER:
        dz = (4 - o) % 4

        @pl.loop(0, features // 256)
        def _(n):
            cols = pl.ds(pl.multiple_of(n * 256, 256), 256)
            mark = place[dz * group : (dz + 1) * group, :]
            got = jnp.dot(mark[:, 0:tok], tokens[:, cols], preferred_element_type=jnp.float32)
            got += jnp.dot(mark[:, tok:], partner_tokens[:, cols], preferred_element_type=jnp.float32)
            outgoing[dz, :, :, cols] = got.astype(jnp.bfloat16).reshape(group // 8, 8, 256)

        for dx in range(4):
            if dz or dx:
                send_zx(dz, dx).start()
            else:
                rows_in[0, 0, 0:3] = outgoing[0, 0:3]

    def start_hop1(o):
        for s in range(4):
            if o or s:
                send_zx((4 - o) % 4, (4 - s) % 4).wait_recv()
        hop1(o, 1, 0).start()
        hop1(o, 0, 1).start()
        hop1(o, 1, 1).start()
        hop1(o, 0, 0).start()

    def start_hop2(o):
        hop1(o, 1, 0).wait_recv()
        hop2(o, 1).start()
        hop1(o, 0, 1).wait_recv()
        hop2(o, 0).start()

    def compute(o):
        hop1(o, 1, 1).wait_recv()
        hop1(o, 0, 0).wait_recv()
        hop2(o, 1).wait_recv()
        hop2(o, 0).wait_recv()
        part_rows = chunk_rows // 4
        for k in range(4):
            lhs[k * part_rows : (k + 1) * part_rows, :] = rows_in[o, k].reshape(part_rows, features)

        @pl.loop(0, hidden.shape[1] // 256)
        def _(n):
            cols = pl.ds(pl.multiple_of(n * 256, 256), 256)
            g = jnp.dot(lhs[...], gate[:, cols], preferred_element_type=jnp.float32)
            u = jnp.dot(lhs[...], up[:, cols], preferred_element_type=jnp.float32)
            hidden[:, cols] = (g / (1.0 + jnp.exp(-g)) * u).astype(jnp.bfloat16)

        @pl.loop(0, features // 256)
        def _(n):
            cols = pl.ds(pl.multiple_of(n * 256, 256), 256)
            p = jnp.dot(hidden[...], down[:, cols], preferred_element_type=jnp.float32)
            partials[o, :, :, :, cols] = p.astype(jnp.bfloat16).reshape(4, part_rows // 8, 8, 256)

        send_far(o, 1).start()
        send_far(o, 0).start()
        send_near(o, 1, 1).start()
        send_near(o, 0, 0).start()

    def add_far(o):
        for up_way in (1, 0):
            half = 0 if up_way else 1
            part = pl.ds(6 * half, 6)
            send_far(o, up_way).wait_recv()
            k = 1 if up_way else 3
            partials[o, k, part] = (
                partials[o, k, part].astype(jnp.float32) + far[o, up_way].astype(jnp.float32)
            ).astype(jnp.bfloat16)
            send_near(o, up_way, half).start()

    def finish(o):
        for up_way in (0, 1):
            for half in (0, 1):
                send_near(o, up_way, half).wait_recv()
        for dx in range(4):
            part = pl.ds(3 * dx, 3)
            total = (
                partials[o, 0, part].astype(jnp.float32)
                + near[o, 0, part].astype(jnp.float32)
                + near[o, 1, part].astype(jnp.float32)
            ).astype(jnp.bfloat16)
            if o or dx:
                partials[o, 0, part] = total
                send_back(o, dx).start()
            else:
                returned[0, 0:3] = total

    start_hop1(ORDER[0])
    start_hop2(ORDER[0])
    start_hop1(ORDER[1])
    for w in weights:
        w.wait()
    for i, o in enumerate(ORDER):
        compute(o)
        if i + 1 < 4:
            start_hop2(ORDER[i + 1])
        if i + 2 < 4:
            start_hop1(ORDER[i + 2])
        if i >= 1:
            add_far(ORDER[i - 1])
        if i >= 2:
            finish(ORDER[i - 2])
    add_far(ORDER[3])
    finish(ORDER[2])
    finish(ORDER[3])

    for v in range(4):
        for s in range(4):
            if v or s:
                send_back((4 - v) % 4, (4 - s) % 4).wait_recv()
    for v in range(4):
        lhs[v * group : (v + 1) * group, :] = returned[v].reshape(group, features)
    slot_lane = lax.broadcasted_iota(jnp.int32, (tok, slots), 1)

    def picks(code):
        return jnp.where(slot_lane == code - core * 1024, 1.0, 0.0).astype(jnp.bfloat16)

    theirs, ours = picks(partner_codes[0:tok, 0:1]), picks(codes[0:tok, 0:1])
    cross_out[...] = jnp.dot(theirs, lhs[...], preferred_element_type=jnp.float32).astype(jnp.bfloat16)
    swap_back = remote(cross_out, cross_in, pair_s.at[2], pair_r.at[2], partner)
    swap_back.start()
    mine = jnp.dot(ours, lhs[...], preferred_element_type=jnp.float32)
    swap_back.wait_recv()
    out[...] = (scores[...] * (mine + cross_in[...].astype(jnp.float32))).astype(jnp.bfloat16)

    swap_tokens.wait_send()
    swap_codes.wait_send()
    swap_back.wait_send()
    for a in range(4):
        for b in range(4):
            if a or b:
                send_zx(a, b).wait_send()
                send_back(a, b).wait_send()
        for way in (0, 1):
            hop2(a, way).wait_send()
            send_far(a, way).wait_send()
            for half in (0, 1):
                hop1(a, way, half).wait_send()
                send_near(a, way, half).wait_send()


def local(tokens, routes, scores, gate_weight, up_weight, down_weight):
    tok, features = tokens.shape
    hid = gate_weight.shape[2]
    slots = 32 * CAP
    group = slots // 4
    bf = jnp.bfloat16
    vmem = pl.BlockSpec(memory_space=pltpu.VMEM)
    hbm = pl.BlockSpec(memory_space=pl.ANY)
    dma = pltpu.SemaphoreType.DMA
    return pl.pallas_call(
        layer,
        out_shape=jax.ShapeDtypeStruct((tok, features), bf),
        in_specs=[vmem] * 4 + [hbm] * 3,
        out_specs=vmem,
        scratch_shapes=[
            pltpu.VMEM((features, hid), bf),
            pltpu.VMEM((features, hid), bf),
            pltpu.VMEM((hid, features), bf),
            pltpu.VMEM((tok + 8, tok), jnp.int32),
            pltpu.VMEM((tok + 8, tok), jnp.int32),
            pltpu.VMEM((tok, features), bf),
            pltpu.VMEM((slots, 2 * tok), bf),
            pltpu.VMEM((4, group // 8, 8, features), bf),
            pltpu.VMEM((4, 4, group // 8, 8, features), bf),
            pltpu.VMEM((slots, features), bf),
            pltpu.VMEM((slots, hid), bf),
            pltpu.VMEM((4, 4, group // 8, 8, features), bf),
            pltpu.VMEM((4, 2, group // 16, 8, features), bf),
            pltpu.VMEM((4, 2, group // 8, 8, features), bf),
            pltpu.VMEM((4, group // 8, 8, features), bf),
            pltpu.VMEM((tok, features), bf),
            pltpu.VMEM((tok, features), bf),
            dma((3,)),
            dma((3,)),
            dma((3,)),
            dma((16,)),
            dma((16,)),
            dma((16,)),
            dma((16,)),
            dma((8,)),
            dma((8,)),
            dma((8,)),
            dma((8,)),
            dma((16,)),
            dma((16,)),
            dma((16,)),
            dma((16,)),
        ],
        compiler_params=pltpu.CompilerParams(
            has_side_effects=True, vmem_limit_bytes=62 * 1024 * 1024
        ),
    )(
        tokens,
        routes.reshape(1, tok),
        routes,
        scores.reshape(tok, 1),
        gate_weight[0],
        up_weight[0],
        down_weight[0],
    )


def solution(mesh):
    in_specs = (
        P(("expert", "etp"), None),
        P(("expert", "etp"), None),
        P(("expert", "etp")),
        P("expert", None, "etp"),
        P("expert", None, "etp"),
        P("expert", "etp", None),
    )
    out_specs = P(("expert", "etp"), None)
    return jax.shard_map(local, mesh=mesh, in_specs=in_specs, out_specs=out_specs, check_vma=False)
```

```python
import jax
import jax.numpy as jnp
from jax import lax
from jax.experimental import pallas as pl
from jax.experimental.pallas import tpu as pltpu
from jax.sharding import PartitionSpec as P

MESH = pl.DeviceIdType.MESH
CAP = 12
ORDER = (0, 1, 3, 2)


def layer(
    tokens,
    routes,
    scores,
    gate_hbm,
    up_hbm,
    down_hbm,
    out,
    gate,
    up,
    down,
    codes,
    other_codes,
    partner_tokens,
    below,
    above,
    place,
    outgoing,
    outgoing_side,
    rows_in,
    lhs,
    hidden,
    partials,
    arrived,
    returned,
    returned_side,
    cross_out,
    cross_in,
    side_out,
    side_in,
    sides,
    home,
    weight_sem,
    pair_s,
    pair_r,
    code_s,
    code_r,
    give_s,
    give_r,
    zx_s,
    zx_r,
    fwd_s,
    fwd_r,
    sum_s,
    sum_r,
    back_s,
    back_r,
    home_s,
    home_r,
):
    e, y = lax.axis_index("expert"), lax.axis_index("etp")
    core, x, z = e % 2, (e // 2) % 4, e // 8
    tok, features = tokens.shape
    half = features // 2
    a, b = pl.ds(0, half), pl.ds(half, half)
    slots = place.shape[1]
    group = slots // 4
    pe = e + 1 - 2 * core
    y_up, y_down = (y + 1) % 4, (y + 3) % 4
    partner, ups, downs = (pe, y), (e, y_up), (e, y_down)

    def owner(dz, dx):
        return ((((z + dz) % 4) * 4 + (x + dx) % 4) * 2 + core, y)

    def remote(src, dst, send, recv, to):
        return pltpu.make_async_remote_copy(
            src_ref=src, dst_ref=dst, send_sem=send, recv_sem=recv, device_id=to, device_id_type=MESH
        )

    weights = [
        pltpu.make_async_copy(gate_hbm, gate, weight_sem.at[0]),
        pltpu.make_async_copy(up_hbm, up, weight_sem.at[1]),
        pltpu.make_async_copy(down_hbm, down, weight_sem.at[2]),
    ]
    code_peers = (partner, ups, (pe, y_up), downs, (pe, y_down))
    barrier = pltpu.get_barrier_semaphore()
    peers = list(code_peers) + [owner(dz, dx) for dz in range(4) for dx in range(4) if dz or dx]
    for peer in peers:
        pl.semaphore_signal(barrier, inc=1, device_id=peer, device_id_type=MESH)
    for w in weights:
        w.start()

    first = lax.broadcasted_iota(jnp.int32, (tok, tok), 0)
    second = lax.broadcasted_iota(jnp.int32, (tok, tok), 1)
    route = routes[...]
    route_rows = jnp.broadcast_to(route.astype(jnp.float32), (tok, tok))
    same = route_rows == route_rows.T
    position = jnp.sum(jnp.where(same & (first < second), 1.0, 0.0), axis=0, keepdims=True)
    chip = ((route // 8 - z) & 3) * 4 + ((route // 2 - x) & 3)
    base = (route & 1) * 1024 + chip * (2 * CAP) + core * CAP
    codes[...] = jnp.broadcast_to(base.astype(jnp.float32) + position, codes.shape)

    pl.semaphore_wait(barrier, len(peers))
    swap_tokens = remote(tokens, partner_tokens, pair_s.at[0], pair_r.at[0], partner)
    swap_tokens.start()
    give_up = remote(tokens.at[:, a], below.at[0], give_s.at[0], give_r.at[0], ups)
    give_down = remote(tokens.at[:, b], above.at[0], give_s.at[1], give_r.at[1], downs)
    give_codes = [
        remote(codes, other_codes.at[i], code_s.at[i], code_r.at[i], peer)
        for i, peer in enumerate(code_peers)
    ]
    for g in give_codes:
        g.start()
    give_up.start()
    give_down.start()

    slot = lax.broadcasted_iota(jnp.int32, (slots, tok), 0)
    shift = core * 1024

    def marks(code):
        return jnp.where(slot == code.astype(jnp.int32) - shift, 1.0, 0.0).astype(jnp.bfloat16)

    place[0, :, 0:tok] = marks(codes[0:1, :])
    for i, (k, c) in enumerate(((0, 1), (1, 0), (1, 1), (2, 0), (2, 1))):
        give_codes[i].wait_recv()
        place[k, :, c * tok : (c + 1) * tok] = marks(other_codes[i, 0:1, :])
    swap_tokens.wait_recv()

    def zx_refs(kind, dz, dx, n):
        o, s = (4 - dz) % 4, (4 - dx) % 4
        src, dst = pl.ds(3 * dx, n), pl.ds(3 * s, n)
        if kind == 0:
            return outgoing.at[dz, src], rows_in.at[o, 0, dst]
        if kind == 1:
            return outgoing_side.at[0, dz, src], rows_in.at[o, 3, dst, :, a]
        return outgoing_side.at[1, dz, src], rows_in.at[o, 1, dst, :, b]

    def send_zx(kind, dz, dx):
        src, dst = zx_refs(kind, dz, dx, 3)
        k = ((4 - dz) % 4) * 3 + kind
        return remote(src, dst, zx_s.at[k], zx_r.at[k], owner(dz, dx))

    def all_zx(kind, o):
        if o:
            refs = zx_refs(kind, (4 - o) % 4, 0, 12)
        else:
            src = outgoing.at[0, pl.ds(3, 9)] if kind == 0 else outgoing_side.at[kind - 1, 0, pl.ds(3, 9)]
            part = pl.ds(3, 9)
            dst = (
                rows_in.at[0, 0, part]
                if kind == 0
                else rows_in.at[0, 3, part, :, a]
                if kind == 1
                else rows_in.at[0, 1, part, :, b]
            )
            refs = src, dst
        k = o * 3 + kind
        return remote(*refs, zx_s.at[k], zx_r.at[k], owner(0, 1))

    def forward(o, k):
        src, dst, to = (
            (rows_in.at[o, 0, :, :, a], rows_in.at[o, 1, :, :, a], downs),
            (rows_in.at[o, 0, :, :, b], rows_in.at[o, 3, :, :, b], ups),
            (rows_in.at[o, 3, :, :, a], rows_in.at[o, 2, :, :, a], ups),
            (rows_in.at[o, 1, :, :, b], rows_in.at[o, 2, :, :, b], downs),
        )[k]
        return remote(src, dst, fwd_s.at[o * 4 + k], fwd_r.at[o * 4 + k], to)

    def send_sum(o, k):
        src, to = (
            (partials.at[o, 1, :, :, a], ups),
            (partials.at[o, 3, :, :, b], downs),
            (partials.at[o, 2, :, :, a], downs),
            (partials.at[o, 2, :, :, b], ups),
        )[k]
        return remote(src, arrived.at[o, k], sum_s.at[o * 4 + k], sum_r.at[o * 4 + k], to)

    def back_refs(kind, o, dx, n):
        v, s = (4 - o) % 4, (4 - dx) % 4
        src, dst = pl.ds(3 * dx, n), pl.ds(3 * s, n)
        if kind == 0:
            return partials.at[o, 0, src], returned.at[v, dst]
        if kind == 1:
            return partials.at[o, 3, src, :, a], returned_side.at[0, v, dst]
        return partials.at[o, 1, src, :, b], returned_side.at[1, v, dst]

    def send_back(kind, o, dx):
        src, dst = back_refs(kind, o, dx, 3)
        k = ((4 - o) % 4) * 3 + kind
        return remote(src, dst, back_s.at[k], back_r.at[k], owner(o, dx))

    def all_back(kind, v):
        if v:
            refs = back_refs(kind, (4 - v) % 4, 0, 12)
        else:
            part = pl.ds(3, 9)
            refs = (
                (partials.at[0, 0, part], returned.at[0, part])
                if kind == 0
                else (partials.at[0, 3, part, :, a], returned_side.at[0, 0, part])
                if kind == 1
                else (partials.at[0, 1, part, :, b], returned_side.at[1, 0, part])
            )
        k = v * 3 + kind
        return remote(*refs, back_s.at[k], back_r.at[k], owner(0, 1))

    def pick(k, dz, mine, theirs):
        mark = place[k, dz * group : (dz + 1) * group, :]
        got = jnp.dot(mark[:, 0:tok], mine, preferred_element_type=jnp.float32)
        got += jnp.dot(mark[:, tok:], theirs, preferred_element_type=jnp.float32)
        return got.astype(jnp.bfloat16).reshape(group // 8, 8, 256)

    def place_own(o):
        dz = (4 - o) % 4

        @pl.loop(0, features // 256)
        def _(n):
            cols = pl.ds(pl.multiple_of(n * 256, 256), 256)
            outgoing[dz, :, :, cols] = pick(0, dz, tokens[:, cols], partner_tokens[:, cols])

        for dx in (1, 3, 2, 0):
            if dz or dx:
                send_zx(0, dz, dx).start()
            else:
                rows_in[0, 0, 0:3] = outgoing[0, 0:3]

    def place_side(o):
        dz = (4 - o) % 4

        @pl.loop(0, half // 256)
        def _(n):
            cols = pl.ds(pl.multiple_of(n * 256, 256), 256)
            outgoing_side[0, dz, :, :, cols] = pick(1, dz, below[0, :, cols], below[1, :, cols])
            outgoing_side[1, dz, :, :, cols] = pick(2, dz, above[0, :, cols], above[1, :, cols])

        for dx in (1, 3, 2, 0):
            if dz or dx:
                send_zx(1, dz, dx).start()
                send_zx(2, dz, dx).start()
            else:
                rows_in[0, 3, 0:3, :, 0:half] = outgoing_side[0, 0, 0:3]
                rows_in[0, 1, 0:3, :, half:] = outgoing_side[1, 0, 0:3]

    def forward_own(o):
        all_zx(0, o).wait_recv()
        forward(o, 0).start()
        forward(o, 1).start()

    def forward_side(o):
        all_zx(1, o).wait_recv()
        forward(o, 2).start()
        all_zx(2, o).wait_recv()
        forward(o, 3).start()

    def compute(o):
        for k in range(4):
            forward(o, k).wait_recv()
        for k in range(4):
            lhs[k * group : (k + 1) * group, :] = rows_in[o, k].reshape(group, features)

        @pl.loop(0, hidden.shape[1] // 256)
        def _(n):
            cols = pl.ds(pl.multiple_of(n * 256, 256), 256)
            g = jnp.dot(lhs[...], gate[:, cols], preferred_element_type=jnp.float32)
            u = jnp.dot(lhs[...], up[:, cols], preferred_element_type=jnp.float32)
            hidden[:, cols] = (g / (1.0 + jnp.exp(-g)) * u).astype(jnp.bfloat16)

        @pl.loop(0, features // 256)
        def _(n):
            cols = pl.ds(pl.multiple_of(n * 256, 256), 256)
            p = jnp.dot(hidden[...], down[:, cols], preferred_element_type=jnp.float32)
            partials[o, :, :, :, cols] = p.astype(jnp.bfloat16).reshape(4, group // 8, 8, 256)

        for k in range(4):
            send_sum(o, k).start()

    def finish(o):
        f32 = jnp.float32

        def added(k, part, cols, which):
            return (partials[o, k, part, :, cols].astype(f32) + arrived[o, which, part].astype(f32)).astype(
                jnp.bfloat16
            )

        for which in range(4):
            send_sum(o, which).wait_recv()
        for dx in (1, 3, 2, 0):
            part = pl.ds(3 * dx, 3)
            partials[o, 0, part, :, a] = added(0, part, a, 0)
            partials[o, 0, part, :, b] = added(0, part, b, 1)
            partials[o, 3, part, :, a] = added(3, part, a, 2)
            partials[o, 1, part, :, b] = added(1, part, b, 3)
            if o or dx:
                for kind in (1, 2, 0):
                    send_back(kind, o, dx).start()
            else:
                returned[0, 0:3] = partials[0, 0, 0:3]
                returned_side[0, 0, 0:3] = partials[0, 3, 0:3, :, 0:half]
                returned_side[1, 0, 0:3] = partials[0, 1, 0:3, :, half:]

    place_own(ORDER[0])
    give_up.wait_recv()
    swap_below = remote(below.at[0], below.at[1], pair_s.at[2], pair_r.at[2], partner)
    swap_below.start()
    give_down.wait_recv()
    swap_above = remote(above.at[0], above.at[1], pair_s.at[3], pair_r.at[3], partner)
    swap_above.start()
    place_own(ORDER[1])
    swap_below.wait_recv()
    swap_above.wait_recv()
    place_side(ORDER[0])
    forward_own(ORDER[0])
    place_own(ORDER[2])
    place_side(ORDER[1])
    forward_own(ORDER[1])
    forward_side(ORDER[0])
    place_own(ORDER[3])
    place_side(ORDER[2])
    place_side(ORDER[3])
    for w in weights:
        w.wait()
    for i, o in enumerate(ORDER):
        compute(o)
        if i + 1 < 4:
            forward_side(ORDER[i + 1])
        if i + 2 < 4:
            forward_own(ORDER[i + 2])
        if i >= 1:
            finish(ORDER[i - 1])
    finish(ORDER[3])

    slot_lane = lax.broadcasted_iota(jnp.int32, (tok, slots), 1)

    def picks(code_row):
        code = jnp.broadcast_to(code_row, (tok, tok)).T[:, 0:1].astype(jnp.int32)
        return jnp.where(slot_lane == code - shift, 1.0, 0.0).astype(jnp.bfloat16)

    def picked(code_row, source):
        return jnp.dot(picks(code_row), source, preferred_element_type=jnp.float32)

    for v in range(4):
        all_back(1, v).wait_recv()
        all_back(2, v).wait_recv()
    for v in range(4):
        rows = slice(v * group, (v + 1) * group)
        lhs[rows, 0:half] = returned_side[0, v].reshape(group, half)
        lhs[rows, half:] = returned_side[1, v].reshape(group, half)
    side_out[0] = picked(other_codes[2, 0:1, :], lhs[:, 0:half]).astype(jnp.bfloat16)
    swap_side_a = remote(side_out.at[0], side_in.at[0], pair_s.at[4], pair_r.at[4], partner)
    swap_side_a.start()
    side_out[1] = picked(other_codes[4, 0:1, :], lhs[:, half:]).astype(jnp.bfloat16)
    swap_side_b = remote(side_out.at[1], side_in.at[1], pair_s.at[5], pair_r.at[5], partner)
    swap_side_b.start()
    mine_a = picked(other_codes[1, 0:1, :], lhs[:, 0:half])
    swap_side_a.wait_recv()
    sides[0] = (mine_a + side_in[0].astype(jnp.float32)).astype(jnp.bfloat16)
    home_down = remote(sides.at[0], home.at[0], home_s.at[0], home_r.at[0], downs)
    home_down.start()
    mine_b = picked(other_codes[3, 0:1, :], lhs[:, half:])
    swap_side_b.wait_recv()
    sides[1] = (mine_b + side_in[1].astype(jnp.float32)).astype(jnp.bfloat16)
    home_up = remote(sides.at[1], home.at[1], home_s.at[1], home_r.at[1], ups)
    home_up.start()
    for v in range(4):
        all_back(0, v).wait_recv()
    for v in range(4):
        lhs[v * group : (v + 1) * group, :] = returned[v].reshape(group, features)
    cross_out[...] = picked(other_codes[0, 0:1, :], lhs[...]).astype(jnp.bfloat16)
    swap_back = remote(cross_out, cross_in, pair_s.at[1], pair_r.at[1], partner)
    swap_back.start()
    mine = picked(codes[0:1, :], lhs[...])
    score = jnp.broadcast_to(scores[...], (tok, tok)).T[:, 0:1]
    swap_back.wait_recv()
    home_down.wait_recv()
    out[:, 0:half] = (
        score * (mine[:, 0:half] + cross_in[:, 0:half].astype(jnp.float32) + home[0].astype(jnp.float32))
    ).astype(jnp.bfloat16)
    home_up.wait_recv()
    out[:, half:] = (
        score * (mine[:, half:] + cross_in[:, half:].astype(jnp.float32) + home[1].astype(jnp.float32))
    ).astype(jnp.bfloat16)

    for c in (
        swap_tokens,
        give_up,
        give_down,
        swap_below,
        swap_above,
        swap_side_a,
        swap_side_b,
        home_down,
        home_up,
        swap_back,
        *give_codes,
    ):
        c.wait_send()
    for o in range(4):
        for kind in range(3):
            all_zx(kind, o).wait_send()
            all_back(kind, o).wait_send()
        for k in range(4):
            forward(o, k).wait_send()
            send_sum(o, k).wait_send()


def local(tokens, routes, scores, gate_weight, up_weight, down_weight):
    tok, features = tokens.shape
    hid = gate_weight.shape[2]
    half = features // 2
    slots = 32 * CAP
    group = slots // 4
    g8 = group // 8
    bf = jnp.bfloat16
    vmem = pl.BlockSpec(memory_space=pltpu.VMEM)
    hbm = pl.BlockSpec(memory_space=pl.ANY)
    sizes = (
        (features, hid),
        (features, hid),
        (hid, features),
        None,
        None,
        (tok, features),
        (2, tok, half),
        (2, tok, half),
        (3, slots, 2 * tok),
        (4, g8, 8, features),
        (2, 4, g8, 8, half),
        (4, 4, g8, 8, features),
        (slots, features),
        (slots, hid),
        (4, 4, g8, 8, features),
        (4, 4, g8, 8, half),
        (4, g8, 8, features),
        (2, 4, g8, 8, half),
        (tok, features),
        (tok, features),
        (2, tok, half),
        (2, tok, half),
        (2, tok, half),
        (2, tok, half),
    )
    scratch = [pltpu.VMEM(s, bf) if s else None for s in sizes]
    scratch[3] = pltpu.VMEM((8, tok), jnp.float32)
    scratch[4] = pltpu.VMEM((5, 8, tok), jnp.float32)
    counts = (3, 6, 6, 5, 5, 2, 2, 12, 12, 16, 16, 16, 16, 12, 12, 2, 2)
    return pl.pallas_call(
        layer,
        out_shape=jax.ShapeDtypeStruct((tok, features), bf),
        in_specs=[vmem] * 3 + [hbm] * 3,
        out_specs=vmem,
        scratch_shapes=scratch + [pltpu.SemaphoreType.DMA((n,)) for n in counts],
        compiler_params=pltpu.CompilerParams(
            collective_id=0, has_side_effects=True, vmem_limit_bytes=62 * 1024 * 1024
        ),
    )(
        tokens,
        routes.reshape(1, tok),
        scores.reshape(1, tok),
        gate_weight[0],
        up_weight[0],
        down_weight[0],
    )


def solution(mesh):
    in_specs = (
        P(("expert", "etp"), None),
        P(("expert", "etp"), None),
        P(("expert", "etp")),
        P("expert", None, "etp"),
        P("expert", None, "etp"),
        P("expert", "etp", None),
    )
    out_specs = P(("expert", "etp"), None)
    return jax.shard_map(local, mesh=mesh, in_specs=in_specs, out_specs=out_specs, check_vma=False)
```

```python
import jax
import jax.numpy as jnp
from jax import lax
from jax.experimental import pallas as pl
from jax.experimental.pallas import tpu as pltpu
from jax.sharding import PartitionSpec as P

MESH = pl.DeviceIdType.MESH
CAP = 12
ORDER = (0, 1, 3, 2)


def layer(
    tokens,
    routes,
    scores,
    gate_hbm,
    up_hbm,
    down_hbm,
    out,
    gate,
    up,
    down,
    codes,
    other_codes,
    partner_tokens,
    below,
    above,
    place,
    outgoing,
    outgoing_side,
    rows_in,
    lhs,
    hidden,
    partials,
    arrived,
    returned,
    returned_side,
    cross_out,
    cross_in,
    side_out,
    side_in,
    sides,
    home,
    passed,
    weight_sem,
    pair_s,
    pair_r,
    code_s,
    code_r,
    give_s,
    give_r,
    zx_s,
    zx_r,
    fwd_s,
    fwd_r,
    sum_s,
    sum_r,
    back_s,
    back_r,
    home_s,
    home_r,
    pass_s,
    pass_r,
):
    e, y = lax.axis_index("expert"), lax.axis_index("etp")
    core, x, z = e % 2, (e // 2) % 4, e // 8
    tok, features = tokens.shape
    half = features // 2
    a, b = pl.ds(0, half), pl.ds(half, half)
    slots = place.shape[1]
    group = slots // 4
    pe = e + 1 - 2 * core
    y_up, y_down = (y + 1) % 4, (y + 3) % 4
    partner, ups, downs = (pe, y), (e, y_up), (e, y_down)

    def owner(dz, dx):
        return ((((z + dz) % 4) * 4 + (x + dx) % 4) * 2 + core, y)

    def remote(src, dst, send, recv, to):
        return pltpu.make_async_remote_copy(
            src_ref=src, dst_ref=dst, send_sem=send, recv_sem=recv, device_id=to, device_id_type=MESH
        )

    weights = [
        pltpu.make_async_copy(gate_hbm, gate, weight_sem.at[0]),
        pltpu.make_async_copy(up_hbm, up, weight_sem.at[1]),
        pltpu.make_async_copy(down_hbm, down, weight_sem.at[2]),
    ]
    code_peers = (partner, ups, (pe, y_up), downs, (pe, y_down))
    barrier = pltpu.get_barrier_semaphore()
    peers = [owner(dz, dx) for dz in range(4) for dx in range(4) if dz or dx] + list(code_peers)
    for peer in peers:
        pl.semaphore_signal(barrier, inc=1, device_id=peer, device_id_type=MESH)
    for w in weights:
        w.start()

    first = lax.broadcasted_iota(jnp.int32, (tok, tok), 0)
    second = lax.broadcasted_iota(jnp.int32, (tok, tok), 1)
    route = routes[...]
    route_rows = jnp.broadcast_to(route.astype(jnp.float32), (tok, tok))
    same = route_rows == route_rows.T
    position = jnp.sum(jnp.where(same & (first < second), 1.0, 0.0), axis=0, keepdims=True)
    chip = ((route // 8 - z) & 3) * 4 + ((route // 2 - x) & 3)
    base = (route & 1) * 1024 + chip * (2 * CAP) + core * CAP
    codes[...] = jnp.broadcast_to(base.astype(jnp.float32) + position, codes.shape)

    pl.semaphore_wait(barrier, len(peers))
    swap_tokens = remote(tokens, partner_tokens, pair_s.at[0], pair_r.at[0], partner)
    swap_tokens.start()
    give_up = remote(tokens.at[:, a], below.at[0], give_s.at[0], give_r.at[0], ups)
    give_down = remote(tokens.at[:, b], above.at[0], give_s.at[1], give_r.at[1], downs)
    give_codes = [
        remote(codes, other_codes.at[i], code_s.at[i], code_r.at[i], peer)
        for i, peer in enumerate(code_peers)
    ]
    for g in give_codes:
        g.start()
    give_up.start()
    give_down.start()

    slot = lax.broadcasted_iota(jnp.int32, (slots, tok), 0)
    shift = core * 1024

    def marks(code):
        return jnp.where(slot == code.astype(jnp.int32) - shift, 1.0, 0.0).astype(jnp.bfloat16)

    place[0, :, 0:tok] = marks(codes[0:1, :])
    for i, (k, c) in enumerate(((0, 1), (1, 0), (1, 1), (2, 0), (2, 1))):
        give_codes[i].wait_recv()
        place[k, :, c * tok : (c + 1) * tok] = marks(other_codes[i, 0:1, :])
    swap_tokens.wait_recv()

    def zx_refs(kind, dz, dx, n):
        o, s = (4 - dz) % 4, (4 - dx) % 4
        src, dst = pl.ds(3 * dx, n), pl.ds(3 * s, n)
        if kind == 0:
            return outgoing.at[dz, src], rows_in.at[o, 0, dst]
        if kind == 1:
            return outgoing_side.at[0, dz, src], rows_in.at[o, 3, dst, :, a]
        return outgoing_side.at[1, dz, src], rows_in.at[o, 1, dst, :, b]

    def send_zx(kind, dz, dx):
        src, dst = zx_refs(kind, dz, dx, 3)
        k = ((4 - dz) % 4) * 3 + kind
        return remote(src, dst, zx_s.at[k], zx_r.at[k], owner(dz, dx))

    def all_zx(kind, o):
        if o:
            refs = zx_refs(kind, (4 - o) % 4, 0, 12)
        else:
            src = outgoing.at[0, pl.ds(3, 9)] if kind == 0 else outgoing_side.at[kind - 1, 0, pl.ds(3, 9)]
            part = pl.ds(3, 9)
            dst = (
                rows_in.at[0, 0, part]
                if kind == 0
                else rows_in.at[0, 3, part, :, a]
                if kind == 1
                else rows_in.at[0, 1, part, :, b]
            )
            refs = src, dst
        k = o * 3 + kind
        return remote(*refs, zx_s.at[k], zx_r.at[k], owner(0, 1))

    def forward(o, k):
        src, dst, to = (
            (rows_in.at[o, 0, :, :, a], rows_in.at[o, 1, :, :, a], downs),
            (rows_in.at[o, 0, :, :, b], rows_in.at[o, 3, :, :, b], ups),
            (rows_in.at[o, 3, :, :, a], rows_in.at[o, 2, :, :, a], ups),
            (rows_in.at[o, 1, :, :, b], rows_in.at[o, 2, :, :, b], downs),
        )[k]
        return remote(src, dst, fwd_s.at[o * 4 + k], fwd_r.at[o * 4 + k], to)

    def send_sum(o, k):
        src, to = (
            (partials.at[o, 1, :, :, a], ups),
            (partials.at[o, 3, :, :, b], downs),
            (partials.at[o, 2, :, :, a], downs),
            (partials.at[o, 2, :, :, b], ups),
        )[k]
        return remote(src, arrived.at[o, k], sum_s.at[o * 4 + k], sum_r.at[o * 4 + k], to)

    def back_refs(kind, o, dx, n):
        v, s = (4 - o) % 4, (4 - dx) % 4
        src, dst = pl.ds(3 * dx, n), pl.ds(3 * s, n)
        if kind == 0:
            return partials.at[o, 0, src], returned.at[v, dst]
        if kind == 1:
            return partials.at[o, 3, src, :, a], returned_side.at[0, v, dst]
        return partials.at[o, 1, src, :, b], returned_side.at[1, v, dst]

    def send_back(kind, o, dx):
        src, dst = back_refs(kind, o, dx, 3)
        k = ((4 - o) % 4) * 3 + kind
        return remote(src, dst, back_s.at[k], back_r.at[k], owner(o, dx))

    def all_back(kind, v):
        if v:
            refs = back_refs(kind, (4 - v) % 4, 0, 12)
        else:
            part = pl.ds(3, 9)
            refs = (
                (partials.at[0, 0, part], returned.at[0, part])
                if kind == 0
                else (partials.at[0, 3, part, :, a], returned_side.at[0, 0, part])
                if kind == 1
                else (partials.at[0, 1, part, :, b], returned_side.at[1, 0, part])
            )
        k = v * 3 + kind
        return remote(*refs, back_s.at[k], back_r.at[k], owner(0, 1))

    def pick(k, dz, mine, theirs):
        mark = place[k, dz * group : (dz + 1) * group, :]
        got = jnp.dot(mark[:, 0:tok], mine, preferred_element_type=jnp.float32)
        got += jnp.dot(mark[:, tok:], theirs, preferred_element_type=jnp.float32)
        return got.astype(jnp.bfloat16).reshape(group // 8, 8, 256)

    def place_own(o):
        dz = (4 - o) % 4

        @pl.loop(0, features // 256)
        def _(n):
            cols = pl.ds(pl.multiple_of(n * 256, 256), 256)
            outgoing[dz, :, :, cols] = pick(0, dz, tokens[:, cols], partner_tokens[:, cols])

        for dx in (1, 3, 2, 0):
            if dz or dx:
                send_zx(0, dz, dx).start()
            else:
                rows_in[0, 0, 0:3] = outgoing[0, 0:3]

    def place_side(o):
        dz = (4 - o) % 4

        @pl.loop(0, half // 256)
        def _(n):
            cols = pl.ds(pl.multiple_of(n * 256, 256), 256)
            outgoing_side[0, dz, :, :, cols] = pick(1, dz, below[0, :, cols], below[1, :, cols])
            outgoing_side[1, dz, :, :, cols] = pick(2, dz, above[0, :, cols], above[1, :, cols])

        for dx in (1, 3, 2, 0):
            if dz or dx:
                send_zx(1, dz, dx).start()
                send_zx(2, dz, dx).start()
            else:
                rows_in[0, 3, 0:3, :, 0:half] = outgoing_side[0, 0, 0:3]
                rows_in[0, 1, 0:3, :, half:] = outgoing_side[1, 0, 0:3]

    def forward_own(o):
        all_zx(0, o).wait_recv()
        forward(o, 0).start()
        forward(o, 1).start()

    def forward_side(o):
        all_zx(1, o).wait_recv()
        forward(o, 2).start()
        all_zx(2, o).wait_recv()
        forward(o, 3).start()

    def compute(o, middle):
        for k in range(4):
            forward(o, k).wait_recv()
        for k in range(4):
            lhs[k * group : (k + 1) * group, :] = rows_in[o, k].reshape(group, features)

        @pl.loop(0, hidden.shape[1] // 256)
        def _(n):
            cols = pl.ds(pl.multiple_of(n * 256, 256), 256)
            g = jnp.dot(lhs[...], gate[:, cols], preferred_element_type=jnp.float32)
            u = jnp.dot(lhs[...], up[:, cols], preferred_element_type=jnp.float32)
            hidden[:, cols] = (g / (1.0 + jnp.exp(-g)) * u).astype(jnp.bfloat16)

        if middle is not None:
            forward_side(middle)

        @pl.loop(0, features // 256)
        def _(n):
            cols = pl.ds(pl.multiple_of(n * 256, 256), 256)
            p = jnp.dot(hidden[...], down[:, cols], preferred_element_type=jnp.float32)
            partials[o, :, :, :, cols] = p.astype(jnp.bfloat16).reshape(4, group // 8, 8, 256)

        for k in range(4):
            send_sum(o, k).start()

    def added(o, k, part, cols, addends):
        total = partials[o, k, part, :, cols].astype(jnp.float32)
        for addend in addends:
            total += addend[part].astype(jnp.float32)
        return total.astype(jnp.bfloat16)

    def finish(o):
        for which in range(4):
            send_sum(o, which).wait_recv()
        for dx in (1, 3, 2, 0):
            part = pl.ds(3 * dx, 3)
            partials[o, 3, part, :, a] = added(o, 3, part, a, [arrived.at[o, 2]])
            partials[o, 1, part, :, b] = added(o, 1, part, b, [arrived.at[o, 3]])
            partials[o, 0, part, :, a] = added(o, 0, part, a, [arrived.at[o, 0]])
            partials[o, 0, part, :, b] = added(o, 0, part, b, [arrived.at[o, 1]])
            if o or dx:
                for kind in (1, 2, 0):
                    send_back(kind, o, dx).start()
            else:
                returned[0, 0:3] = partials[0, 0, 0:3]
                returned_side[0, 0, 0:3] = partials[0, 3, 0:3, :, 0:half]
                returned_side[1, 0, 0:3] = partials[0, 1, 0:3, :, half:]

    last = ORDER[3]
    pass_down = remote(partials.at[last, 3, :, :, a], passed.at[0], pass_s.at[0], pass_r.at[0], downs)
    pass_up = remote(partials.at[last, 1, :, :, b], passed.at[1], pass_s.at[1], pass_r.at[1], ups)

    def pass_sums():
        everything = pl.ds(0, group // 8)
        send_sum(last, 2).wait_recv()
        partials[last, 3, :, :, a] = added(last, 3, everything, a, [arrived.at[last, 2]])
        pass_down.start()
        send_sum(last, 3).wait_recv()
        partials[last, 1, :, :, b] = added(last, 1, everything, b, [arrived.at[last, 3]])
        pass_up.start()

    def finish_last():
        send_sum(last, 0).wait_recv()
        send_sum(last, 1).wait_recv()
        pass_down.wait_recv()
        pass_up.wait_recv()
        for dx in (1, 3, 2, 0):
            part = pl.ds(3 * dx, 3)
            partials[last, 0, part, :, a] = added(last, 0, part, a, [arrived.at[last, 0], passed.at[0]])
            partials[last, 0, part, :, b] = added(last, 0, part, b, [arrived.at[last, 1], passed.at[1]])
            send_back(0, last, dx).start()

    place_own(ORDER[0])
    place_own(ORDER[1])
    forward_own(ORDER[0])
    give_up.wait_recv()
    swap_below = remote(below.at[0], below.at[1], pair_s.at[2], pair_r.at[2], partner)
    swap_below.start()
    give_down.wait_recv()
    swap_above = remote(above.at[0], above.at[1], pair_s.at[3], pair_r.at[3], partner)
    swap_above.start()
    place_own(ORDER[2])
    swap_below.wait_recv()
    swap_above.wait_recv()
    place_side(ORDER[0])
    place_side(ORDER[1])
    forward_own(ORDER[1])
    place_own(ORDER[3])
    forward_side(ORDER[0])
    place_side(ORDER[2])
    place_side(ORDER[3])
    for w in weights:
        w.wait()
    for i, o in enumerate(ORDER):
        if i + 2 < 4:
            forward_own(ORDER[i + 2])
        compute(o, ORDER[i + 1] if i + 1 < 4 else None)
        if i >= 1:
            finish(ORDER[i - 1])
    pass_sums()

    slot_lane = lax.broadcasted_iota(jnp.int32, (tok, slots), 1)

    def picks(code_row):
        code = jnp.broadcast_to(code_row, (tok, tok)).T[:, 0:1].astype(jnp.int32)
        return jnp.where(slot_lane == code - shift, 1.0, 0.0).astype(jnp.bfloat16)

    def picked(code_row, source):
        return jnp.dot(picks(code_row), source, preferred_element_type=jnp.float32)

    for o in ORDER[:3]:
        all_back(1, (4 - o) % 4).wait_recv()
        all_back(2, (4 - o) % 4).wait_recv()
    unused = (4 - last) % 4
    returned_side[:, unused] = jnp.zeros((2, group // 8, 8, half), jnp.bfloat16)
    for v in range(4):
        rows = slice(v * group, (v + 1) * group)
        lhs[rows, 0:half] = returned_side[0, v].reshape(group, half)
        lhs[rows, half:] = returned_side[1, v].reshape(group, half)
    side_out[0] = picked(other_codes[2, 0:1, :], lhs[:, 0:half]).astype(jnp.bfloat16)
    swap_side_a = remote(side_out.at[0], side_in.at[0], pair_s.at[4], pair_r.at[4], partner)
    swap_side_a.start()
    side_out[1] = picked(other_codes[4, 0:1, :], lhs[:, half:]).astype(jnp.bfloat16)
    swap_side_b = remote(side_out.at[1], side_in.at[1], pair_s.at[5], pair_r.at[5], partner)
    swap_side_b.start()
    mine_a = picked(other_codes[1, 0:1, :], lhs[:, 0:half])
    swap_side_a.wait_recv()
    sides[0] = (mine_a + side_in[0].astype(jnp.float32)).astype(jnp.bfloat16)
    home_down = remote(sides.at[0], home.at[0], home_s.at[0], home_r.at[0], downs)
    home_down.start()
    mine_b = picked(other_codes[3, 0:1, :], lhs[:, half:])
    swap_side_b.wait_recv()
    sides[1] = (mine_b + side_in[1].astype(jnp.float32)).astype(jnp.bfloat16)
    home_up = remote(sides.at[1], home.at[1], home_s.at[1], home_r.at[1], ups)
    home_up.start()
    finish_last()
    for v in range(4):
        all_back(0, v).wait_recv()
    for v in range(4):
        lhs[v * group : (v + 1) * group, :] = returned[v].reshape(group, features)
    cross_out[...] = picked(other_codes[0, 0:1, :], lhs[...]).astype(jnp.bfloat16)
    swap_back = remote(cross_out, cross_in, pair_s.at[1], pair_r.at[1], partner)
    swap_back.start()
    mine = picked(codes[0:1, :], lhs[...])
    score = jnp.broadcast_to(scores[...], (tok, tok)).T[:, 0:1]
    swap_back.wait_recv()
    home_down.wait_recv()
    out[:, 0:half] = (
        score * (mine[:, 0:half] + cross_in[:, 0:half].astype(jnp.float32) + home[0].astype(jnp.float32))
    ).astype(jnp.bfloat16)
    home_up.wait_recv()
    out[:, half:] = (
        score * (mine[:, half:] + cross_in[:, half:].astype(jnp.float32) + home[1].astype(jnp.float32))
    ).astype(jnp.bfloat16)

    for c in (
        swap_tokens,
        give_up,
        give_down,
        swap_below,
        swap_above,
        swap_side_a,
        swap_side_b,
        home_down,
        home_up,
        swap_back,
        pass_down,
        pass_up,
        *give_codes,
    ):
        c.wait_send()
    for o in range(4):
        for kind in range(3):
            all_zx(kind, o).wait_send()
            if kind == 0 or o != unused:
                all_back(kind, o).wait_send()
        for k in range(4):
            forward(o, k).wait_send()
            send_sum(o, k).wait_send()


def local(tokens, routes, scores, gate_weight, up_weight, down_weight):
    tok, features = tokens.shape
    hid = gate_weight.shape[2]
    half = features // 2
    slots = 32 * CAP
    group = slots // 4
    g8 = group // 8
    bf = jnp.bfloat16
    vmem = pl.BlockSpec(memory_space=pltpu.VMEM)
    hbm = pl.BlockSpec(memory_space=pl.ANY)
    sizes = (
        (features, hid),
        (features, hid),
        (hid, features),
        None,
        None,
        (tok, features),
        (2, tok, half),
        (2, tok, half),
        (3, slots, 2 * tok),
        (4, g8, 8, features),
        (2, 4, g8, 8, half),
        (4, 4, g8, 8, features),
        (slots, features),
        (slots, hid),
        (4, 4, g8, 8, features),
        (4, 4, g8, 8, half),
        (4, g8, 8, features),
        (2, 4, g8, 8, half),
        (tok, features),
        (tok, features),
        (2, tok, half),
        (2, tok, half),
        (2, tok, half),
        (2, tok, half),
        (2, g8, 8, half),
    )
    scratch = [pltpu.VMEM(s, bf) if s else None for s in sizes]
    scratch[3] = pltpu.VMEM((8, tok), jnp.float32)
    scratch[4] = pltpu.VMEM((5, 8, tok), jnp.float32)
    counts = (3, 6, 6, 5, 5, 2, 2, 12, 12, 16, 16, 16, 16, 12, 12, 2, 2, 2, 2)
    return pl.pallas_call(
        layer,
        out_shape=jax.ShapeDtypeStruct((tok, features), bf),
        in_specs=[vmem] * 3 + [hbm] * 3,
        out_specs=vmem,
        scratch_shapes=scratch + [pltpu.SemaphoreType.DMA((n,)) for n in counts],
        compiler_params=pltpu.CompilerParams(
            collective_id=0, has_side_effects=True, vmem_limit_bytes=62 * 1024 * 1024
        ),
    )(
        tokens,
        routes.reshape(1, tok),
        scores.reshape(1, tok),
        gate_weight[0],
        up_weight[0],
        down_weight[0],
    )


def solution(mesh):
    in_specs = (
        P(("expert", "etp"), None),
        P(("expert", "etp"), None),
        P(("expert", "etp")),
        P("expert", None, "etp"),
        P("expert", None, "etp"),
        P("expert", "etp", None),
    )
    out_specs = P(("expert", "etp"), None)
    return jax.shard_map(local, mesh=mesh, in_specs=in_specs, out_specs=out_specs, check_vma=False)
```

```python
import jax
import jax.numpy as jnp
from jax import lax
from jax.experimental import pallas as pl
from jax.experimental.pallas import tpu as pltpu
from jax.sharding import PartitionSpec as P

MESH = pl.DeviceIdType.MESH
CAP = 12
ORDER = (0, 1, 3, 2)


def layer(
    tokens,
    routes,
    scores,
    gate_hbm,
    up_hbm,
    down_hbm,
    out,
    gate,
    up,
    down,
    codes,
    other_codes,
    partner_tokens,
    below,
    above,
    place,
    outgoing,
    outgoing_side,
    rows_in,
    lhs,
    hidden,
    partials,
    arrived,
    returned,
    returned_side,
    cross_out,
    cross_in,
    side_out,
    side_in,
    sides,
    home,
    passed,
    weight_sem,
    pair_s,
    pair_r,
    code_s,
    code_r,
    give_s,
    give_r,
    zx_s,
    zx_r,
    fwd_s,
    fwd_r,
    sum_s,
    sum_r,
    back_s,
    back_r,
    home_s,
    home_r,
    pass_s,
    pass_r,
):
    e, y = lax.axis_index("expert"), lax.axis_index("etp")
    core, x, z = e % 2, (e // 2) % 4, e // 8
    tok, features = tokens.shape
    half = features // 2
    a, b = pl.ds(0, half), pl.ds(half, half)
    slots = place.shape[1]
    group = slots // 4
    pe = e + 1 - 2 * core
    y_up, y_down = (y + 1) % 4, (y + 3) % 4
    partner, ups, downs = (pe, y), (e, y_up), (e, y_down)

    def owner(dz, dx):
        return ((((z + dz + dx) % 4) * 4 + (x + dx) % 4) * 2 + core, y)

    def remote(src, dst, send, recv, to):
        return pltpu.make_async_remote_copy(
            src_ref=src, dst_ref=dst, send_sem=send, recv_sem=recv, device_id=to, device_id_type=MESH
        )

    weights = [
        pltpu.make_async_copy(gate_hbm, gate, weight_sem.at[0]),
        pltpu.make_async_copy(up_hbm, up, weight_sem.at[1]),
        pltpu.make_async_copy(down_hbm, down, weight_sem.at[2]),
    ]
    code_peers = (partner, ups, (pe, y_up), downs, (pe, y_down))
    barrier = pltpu.get_barrier_semaphore()
    peers = [owner(dz, dx) for dz in range(4) for dx in range(4) if dz or dx] + list(code_peers)
    for peer in peers:
        pl.semaphore_signal(barrier, inc=1, device_id=peer, device_id_type=MESH)
    for w in weights:
        w.start()

    first = lax.broadcasted_iota(jnp.int32, (tok, tok), 0)
    second = lax.broadcasted_iota(jnp.int32, (tok, tok), 1)
    route = routes[...]
    route_rows = jnp.broadcast_to(route.astype(jnp.float32), (tok, tok))
    same = route_rows == route_rows.T
    position = jnp.sum(jnp.where(same & (first < second), 1.0, 0.0), axis=0, keepdims=True)
    chip_x = (route // 2 - x) & 3
    chip = ((route // 8 - z - chip_x) & 3) * 4 + chip_x
    base = (route & 1) * 1024 + chip * (2 * CAP) + core * CAP
    codes[...] = jnp.broadcast_to(base.astype(jnp.float32) + position, codes.shape)

    pl.semaphore_wait(barrier, len(peers))
    swap_tokens = remote(tokens, partner_tokens, pair_s.at[0], pair_r.at[0], partner)
    swap_tokens.start()
    give_up = remote(tokens.at[:, a], below.at[0], give_s.at[0], give_r.at[0], ups)
    give_down = remote(tokens.at[:, b], above.at[0], give_s.at[1], give_r.at[1], downs)
    give_codes = [
        remote(codes, other_codes.at[i], code_s.at[i], code_r.at[i], peer)
        for i, peer in enumerate(code_peers)
    ]
    for g in give_codes:
        g.start()
    give_up.start()
    give_down.start()

    slot = lax.broadcasted_iota(jnp.int32, (slots, tok), 0)
    shift = core * 1024

    def marks(code):
        return jnp.where(slot == code.astype(jnp.int32) - shift, 1.0, 0.0).astype(jnp.bfloat16)

    place[0, :, 0:tok] = marks(codes[0:1, :])
    for i, (k, c) in enumerate(((0, 1), (1, 0), (1, 1), (2, 0), (2, 1))):
        give_codes[i].wait_recv()
        place[k, :, c * tok : (c + 1) * tok] = marks(other_codes[i, 0:1, :])
    swap_tokens.wait_recv()

    def zx_refs(kind, dz, dx, n):
        o, s = (4 - dz) % 4, (4 - dx) % 4
        src, dst = pl.ds(3 * dx, n), pl.ds(3 * s, n)
        if kind == 0:
            return outgoing.at[dz, src], rows_in.at[o, 0, dst]
        if kind == 1:
            return outgoing_side.at[0, dz, src], rows_in.at[o, 3, dst, :, a]
        return outgoing_side.at[1, dz, src], rows_in.at[o, 1, dst, :, b]

    def send_zx(kind, dz, dx):
        src, dst = zx_refs(kind, dz, dx, 3)
        k = ((4 - dz) % 4) * 3 + kind
        return remote(src, dst, zx_s.at[k], zx_r.at[k], owner(dz, dx))

    def all_zx(kind, o):
        if o:
            refs = zx_refs(kind, (4 - o) % 4, 0, 12)
        else:
            src = outgoing.at[0, pl.ds(3, 9)] if kind == 0 else outgoing_side.at[kind - 1, 0, pl.ds(3, 9)]
            part = pl.ds(3, 9)
            dst = (
                rows_in.at[0, 0, part]
                if kind == 0
                else rows_in.at[0, 3, part, :, a]
                if kind == 1
                else rows_in.at[0, 1, part, :, b]
            )
            refs = src, dst
        k = o * 3 + kind
        return remote(*refs, zx_s.at[k], zx_r.at[k], owner(0, 1))

    def forward(o, k):
        src, dst, to = (
            (rows_in.at[o, 0, :, :, a], rows_in.at[o, 1, :, :, a], downs),
            (rows_in.at[o, 0, :, :, b], rows_in.at[o, 3, :, :, b], ups),
            (rows_in.at[o, 3, :, :, a], rows_in.at[o, 2, :, :, a], ups),
            (rows_in.at[o, 1, :, :, b], rows_in.at[o, 2, :, :, b], downs),
        )[k]
        return remote(src, dst, fwd_s.at[o * 4 + k], fwd_r.at[o * 4 + k], to)

    def send_sum(o, k):
        src, to = (
            (partials.at[o, 1, :, :, a], ups),
            (partials.at[o, 3, :, :, b], downs),
            (partials.at[o, 2, :, :, a], downs),
            (partials.at[o, 2, :, :, b], ups),
        )[k]
        return remote(src, arrived.at[o, k], sum_s.at[o * 4 + k], sum_r.at[o * 4 + k], to)

    def back_refs(kind, o, dx, n):
        v, s = (4 - o) % 4, (4 - dx) % 4
        src, dst = pl.ds(3 * dx, n), pl.ds(3 * s, n)
        if kind == 0:
            return partials.at[o, 0, src], returned.at[v, dst]
        if kind == 1:
            return partials.at[o, 3, src, :, a], returned_side.at[0, v, dst]
        return partials.at[o, 1, src, :, b], returned_side.at[1, v, dst]

    def send_back(kind, o, dx):
        src, dst = back_refs(kind, o, dx, 3)
        k = ((4 - o) % 4) * 3 + kind
        return remote(src, dst, back_s.at[k], back_r.at[k], owner(o, dx))

    def all_back(kind, v):
        if v:
            refs = back_refs(kind, (4 - v) % 4, 0, 12)
        else:
            part = pl.ds(3, 9)
            refs = (
                (partials.at[0, 0, part], returned.at[0, part])
                if kind == 0
                else (partials.at[0, 3, part, :, a], returned_side.at[0, 0, part])
                if kind == 1
                else (partials.at[0, 1, part, :, b], returned_side.at[1, 0, part])
            )
        k = v * 3 + kind
        return remote(*refs, back_s.at[k], back_r.at[k], owner(0, 1))

    def pick(k, dz, mine, theirs):
        mark = place[k, dz * group : (dz + 1) * group, :]
        got = jnp.dot(mark[:, 0:tok], mine, preferred_element_type=jnp.float32)
        got += jnp.dot(mark[:, tok:], theirs, preferred_element_type=jnp.float32)
        return got.astype(jnp.bfloat16).reshape(group // 8, 8, 256)

    def place_own(o):
        dz = (4 - o) % 4

        @pl.loop(0, features // 256)
        def _(n):
            cols = pl.ds(pl.multiple_of(n * 256, 256), 256)
            outgoing[dz, :, :, cols] = pick(0, dz, tokens[:, cols], partner_tokens[:, cols])

        for dx in (2, 1, 3, 0):
            if dz or dx:
                send_zx(0, dz, dx).start()
            else:
                rows_in[0, 0, 0:3] = outgoing[0, 0:3]

    def place_side(o):
        dz = (4 - o) % 4

        @pl.loop(0, half // 256)
        def _(n):
            cols = pl.ds(pl.multiple_of(n * 256, 256), 256)
            outgoing_side[0, dz, :, :, cols] = pick(1, dz, below[0, :, cols], below[1, :, cols])
            outgoing_side[1, dz, :, :, cols] = pick(2, dz, above[0, :, cols], above[1, :, cols])

        for dx in (2, 1, 3, 0):
            if dz or dx:
                send_zx(1, dz, dx).start()
                send_zx(2, dz, dx).start()
            else:
                rows_in[0, 3, 0:3, :, 0:half] = outgoing_side[0, 0, 0:3]
                rows_in[0, 1, 0:3, :, half:] = outgoing_side[1, 0, 0:3]

    def forward_own(o):
        all_zx(0, o).wait_recv()
        forward(o, 0).start()
        forward(o, 1).start()

    def forward_side(o):
        all_zx(1, o).wait_recv()
        forward(o, 2).start()
        all_zx(2, o).wait_recv()
        forward(o, 3).start()

    def compute(o, middle):
        for k in range(4):
            forward(o, k).wait_recv()
        for k in range(4):
            lhs[k * group : (k + 1) * group, :] = rows_in[o, k].reshape(group, features)

        @pl.loop(0, hidden.shape[1] // 256)
        def _(n):
            cols = pl.ds(pl.multiple_of(n * 256, 256), 256)
            g = jnp.dot(lhs[...], gate[:, cols], preferred_element_type=jnp.float32)
            u = jnp.dot(lhs[...], up[:, cols], preferred_element_type=jnp.float32)
            hidden[:, cols] = (g / (1.0 + jnp.exp(-g)) * u).astype(jnp.bfloat16)

        if middle is not None:
            forward_side(middle)

        @pl.loop(0, features // 256)
        def _(n):
            cols = pl.ds(pl.multiple_of(n * 256, 256), 256)
            p = jnp.dot(hidden[...], down[:, cols], preferred_element_type=jnp.float32)
            partials[o, :, :, :, cols] = p.astype(jnp.bfloat16).reshape(4, group // 8, 8, 256)

        for k in (2, 3, 0, 1):
            send_sum(o, k).start()

    def added(o, k, part, cols, addends):
        total = partials[o, k, part, :, cols].astype(jnp.float32)
        for addend in addends:
            total += addend[part].astype(jnp.float32)
        return total.astype(jnp.bfloat16)

    def finish(o):
        for which in range(4):
            send_sum(o, which).wait_recv()
        for dx in (2, 1, 3, 0):
            part = pl.ds(3 * dx, 3)
            partials[o, 3, part, :, a] = added(o, 3, part, a, [arrived.at[o, 2]])
            partials[o, 1, part, :, b] = added(o, 1, part, b, [arrived.at[o, 3]])
            partials[o, 0, part, :, a] = added(o, 0, part, a, [arrived.at[o, 0]])
            partials[o, 0, part, :, b] = added(o, 0, part, b, [arrived.at[o, 1]])
            if o or dx:
                for kind in (1, 2, 0):
                    send_back(kind, o, dx).start()
            else:
                returned[0, 0:3] = partials[0, 0, 0:3]
                returned_side[0, 0, 0:3] = partials[0, 3, 0:3, :, 0:half]
                returned_side[1, 0, 0:3] = partials[0, 1, 0:3, :, half:]

    last = ORDER[3]
    unused = (4 - last) % 4
    pass_down = remote(partials.at[last, 3, :, :, a], passed.at[0], pass_s.at[0], pass_r.at[0], downs)
    pass_up = remote(partials.at[last, 1, :, :, b], passed.at[1], pass_s.at[1], pass_r.at[1], ups)

    def pass_sums():
        everything = pl.ds(0, group // 8)
        send_sum(last, 2).wait_recv()
        partials[last, 3, :, :, a] = added(last, 3, everything, a, [arrived.at[last, 2]])
        pass_down.start()
        send_sum(last, 3).wait_recv()
        partials[last, 1, :, :, b] = added(last, 1, everything, b, [arrived.at[last, 3]])
        pass_up.start()

    def finish_last():
        send_sum(last, 0).wait_recv()
        send_sum(last, 1).wait_recv()
        pass_down.wait_recv()
        pass_up.wait_recv()
        for dx in (2, 1, 3, 0):
            part = pl.ds(3 * dx, 3)
            partials[last, 0, part, :, a] = added(last, 0, part, a, [arrived.at[last, 0], passed.at[0]])
            partials[last, 0, part, :, b] = added(last, 0, part, b, [arrived.at[last, 1], passed.at[1]])
            send_back(0, last, dx).start()

    place_own(ORDER[0])
    place_own(ORDER[1])
    forward_own(ORDER[0])
    give_up.wait_recv()
    swap_below = remote(below.at[0], below.at[1], pair_s.at[2], pair_r.at[2], partner)
    swap_below.start()
    give_down.wait_recv()
    swap_above = remote(above.at[0], above.at[1], pair_s.at[3], pair_r.at[3], partner)
    swap_above.start()
    place_own(ORDER[2])
    swap_below.wait_recv()
    swap_above.wait_recv()
    place_side(ORDER[0])
    place_side(ORDER[1])
    forward_own(ORDER[1])
    place_own(ORDER[3])
    forward_side(ORDER[0])
    place_side(ORDER[2])
    place_side(ORDER[3])
    for w in weights:
        w.wait()
    for i, o in enumerate(ORDER):
        if i + 2 < 4:
            forward_own(ORDER[i + 2])
        compute(o, ORDER[i + 1] if i + 1 < 4 else None)
        if i >= 1:
            finish(ORDER[i - 1])
    pass_sums()

    slot_lane = lax.broadcasted_iota(jnp.int32, (tok, slots), 1)

    def picks(code_row):
        code = jnp.broadcast_to(code_row, (tok, tok)).T[:, 0:1].astype(jnp.int32)
        return jnp.where(slot_lane == code - shift, 1.0, 0.0).astype(jnp.bfloat16)

    def picked(code_row, source):
        return jnp.dot(picks(code_row), source, preferred_element_type=jnp.float32)

    def picked_last(code_row, source):
        return jnp.dot(
            picks(code_row)[:, unused * group : (unused + 1) * group], source, preferred_element_type=jnp.float32
        )

    for o in ORDER[:3]:
        all_back(1, (4 - o) % 4).wait_recv()
        all_back(2, (4 - o) % 4).wait_recv()
    returned_side[:, unused] = jnp.zeros((2, group // 8, 8, half), jnp.bfloat16)
    for v in range(4):
        rows = slice(v * group, (v + 1) * group)
        lhs[rows, 0:half] = returned_side[0, v].reshape(group, half)
        lhs[rows, half:] = returned_side[1, v].reshape(group, half)
    side_out[0] = picked(other_codes[2, 0:1, :], lhs[:, 0:half]).astype(jnp.bfloat16)
    swap_side_a = remote(side_out.at[0], side_in.at[0], pair_s.at[4], pair_r.at[4], partner)
    swap_side_a.start()
    side_out[1] = picked(other_codes[4, 0:1, :], lhs[:, half:]).astype(jnp.bfloat16)
    swap_side_b = remote(side_out.at[1], side_in.at[1], pair_s.at[5], pair_r.at[5], partner)
    swap_side_b.start()
    mine_a = picked(other_codes[1, 0:1, :], lhs[:, 0:half])
    swap_side_a.wait_recv()
    sides[0] = (mine_a + side_in[0].astype(jnp.float32)).astype(jnp.bfloat16)
    home_down = remote(sides.at[0], home.at[0], home_s.at[0], home_r.at[0], downs)
    home_down.start()
    mine_b = picked(other_codes[3, 0:1, :], lhs[:, half:])
    swap_side_b.wait_recv()
    sides[1] = (mine_b + side_in[1].astype(jnp.float32)).astype(jnp.bfloat16)
    home_up = remote(sides.at[1], home.at[1], home_s.at[1], home_r.at[1], ups)
    home_up.start()
    for o in ORDER[:3]:
        all_back(0, (4 - o) % 4).wait_recv()
    for v in range(4):
        rows = slice(v * group, (v + 1) * group)
        lhs[rows, :] = jnp.zeros((group, features), lhs.dtype) if v == unused else returned[v].reshape(group, features)
    theirs = picked(other_codes[0, 0:1, :], lhs[...])
    mine = picked(codes[0:1, :], lhs[...])
    finish_last()
    all_back(0, unused).wait_recv()
    lhs[0:group, :] = returned[unused].reshape(group, features)
    theirs += picked_last(other_codes[0, 0:1, :], lhs[0:group, :])
    cross_out[...] = theirs.astype(jnp.bfloat16)
    swap_back = remote(cross_out, cross_in, pair_s.at[1], pair_r.at[1], partner)
    swap_back.start()
    mine += picked_last(codes[0:1, :], lhs[0:group, :])
    score = jnp.broadcast_to(scores[...], (tok, tok)).T[:, 0:1]
    swap_back.wait_recv()
    home_down.wait_recv()
    out[:, 0:half] = (
        score * (mine[:, 0:half] + cross_in[:, 0:half].astype(jnp.float32) + home[0].astype(jnp.float32))
    ).astype(jnp.bfloat16)
    home_up.wait_recv()
    out[:, half:] = (
        score * (mine[:, half:] + cross_in[:, half:].astype(jnp.float32) + home[1].astype(jnp.float32))
    ).astype(jnp.bfloat16)

    for c in (
        swap_tokens,
        give_up,
        give_down,
        swap_below,
        swap_above,
        swap_side_a,
        swap_side_b,
        home_down,
        home_up,
        swap_back,
        pass_down,
        pass_up,
        *give_codes,
    ):
        c.wait_send()
    for o in range(4):
        for kind in range(3):
            all_zx(kind, o).wait_send()
            if kind == 0 or o != unused:
                all_back(kind, o).wait_send()
        for k in range(4):
            forward(o, k).wait_send()
            send_sum(o, k).wait_send()


def local(tokens, routes, scores, gate_weight, up_weight, down_weight):
    tok, features = tokens.shape
    hid = gate_weight.shape[2]
    half = features // 2
    slots = 32 * CAP
    group = slots // 4
    g8 = group // 8
    bf = jnp.bfloat16
    vmem = pl.BlockSpec(memory_space=pltpu.VMEM)
    hbm = pl.BlockSpec(memory_space=pl.ANY)
    sizes = (
        (features, hid),
        (features, hid),
        (hid, features),
        None,
        None,
        (tok, features),
        (2, tok, half),
        (2, tok, half),
        (3, slots, 2 * tok),
        (4, g8, 8, features),
        (2, 4, g8, 8, half),
        (4, 4, g8, 8, features),
        (slots, features),
        (slots, hid),
        (4, 4, g8, 8, features),
        (4, 4, g8, 8, half),
        (4, g8, 8, features),
        (2, 4, g8, 8, half),
        (tok, features),
        (tok, features),
        (2, tok, half),
        (2, tok, half),
        (2, tok, half),
        (2, tok, half),
        (2, g8, 8, half),
    )
    scratch = [pltpu.VMEM(s, bf) if s else None for s in sizes]
    scratch[3] = pltpu.VMEM((8, tok), jnp.float32)
    scratch[4] = pltpu.VMEM((5, 8, tok), jnp.float32)
    counts = (3, 6, 6, 5, 5, 2, 2, 12, 12, 16, 16, 16, 16, 12, 12, 2, 2, 2, 2)
    return pl.pallas_call(
        layer,
        out_shape=jax.ShapeDtypeStruct((tok, features), bf),
        in_specs=[vmem] * 3 + [hbm] * 3,
        out_specs=vmem,
        scratch_shapes=scratch + [pltpu.SemaphoreType.DMA((n,)) for n in counts],
        compiler_params=pltpu.CompilerParams(
            collective_id=0, has_side_effects=True, vmem_limit_bytes=62 * 1024 * 1024
        ),
    )(
        tokens,
        routes.reshape(1, tok),
        scores.reshape(1, tok),
        gate_weight[0],
        up_weight[0],
        down_weight[0],
    )


def solution(mesh):
    in_specs = (
        P(("expert", "etp"), None),
        P(("expert", "etp"), None),
        P(("expert", "etp")),
        P("expert", None, "etp"),
        P("expert", None, "etp"),
        P("expert", "etp", None),
    )
    out_specs = P(("expert", "etp"), None)
    return jax.shard_map(local, mesh=mesh, in_specs=in_specs, out_specs=out_specs, check_vma=False)
```

```python
import jax
import jax.numpy as jnp
from jax import lax
from jax.experimental import pallas as pl
from jax.experimental.pallas import tpu as pltpu
from jax.sharding import PartitionSpec as P

MESH = pl.DeviceIdType.MESH
CAP = 12
ORDER = (0, 1, 3, 2)


def layer(
    tokens,
    routes,
    scores,
    gate_hbm,
    up_hbm,
    down_hbm,
    out,
    gate,
    up,
    down,
    codes,
    other_codes,
    partner_tokens,
    below,
    above,
    place,
    outgoing,
    outgoing_side,
    rows_in,
    lhs,
    hidden,
    partials,
    arrived,
    returned,
    returned_side,
    cross_out,
    cross_in,
    side_out,
    side_in,
    sides,
    home,
    passed,
    weight_sem,
    pair_s,
    pair_r,
    code_s,
    code_r,
    give_s,
    give_r,
    zx_s,
    zx_r,
    fwd_s,
    fwd_r,
    sum_s,
    sum_r,
    back_s,
    back_r,
    home_s,
    home_r,
    pass_s,
    pass_r,
):
    e, y = lax.axis_index("expert"), lax.axis_index("etp")
    core, x, z = e % 2, (e // 2) % 4, e // 8
    tok, features = tokens.shape
    half = features // 2
    a, b = pl.ds(0, half), pl.ds(half, half)
    slots = place.shape[1]
    group = slots // 4
    pe = e + 1 - 2 * core
    y_up, y_down = (y + 1) % 4, (y + 3) % 4
    partner, ups, downs = (pe, y), (e, y_up), (e, y_down)

    def owner(dz, dx):
        return ((((z + dz + dx) % 4) * 4 + (x + dx) % 4) * 2 + core, y)

    def remote(src, dst, send, recv, to):
        return pltpu.make_async_remote_copy(
            src_ref=src, dst_ref=dst, send_sem=send, recv_sem=recv, device_id=to, device_id_type=MESH
        )

    weights = [
        pltpu.make_async_copy(gate_hbm, gate, weight_sem.at[0]),
        pltpu.make_async_copy(up_hbm, up, weight_sem.at[1]),
        pltpu.make_async_copy(down_hbm, down, weight_sem.at[2]),
    ]
    code_peers = (partner, ups, (pe, y_up), downs, (pe, y_down))
    barrier = pltpu.get_barrier_semaphore()
    peers = [owner(dz, dx) for dz in range(4) for dx in range(4) if dz or dx] + list(code_peers)
    for peer in peers:
        pl.semaphore_signal(barrier, inc=1, device_id=peer, device_id_type=MESH)
    for w in weights:
        w.start()

    first = lax.broadcasted_iota(jnp.int32, (tok, tok), 0)
    second = lax.broadcasted_iota(jnp.int32, (tok, tok), 1)
    route = routes[...]
    route_rows = jnp.broadcast_to(route.astype(jnp.float32), (tok, tok))
    same = route_rows == route_rows.T
    position = jnp.sum(jnp.where(same & (first < second), 1.0, 0.0), axis=0, keepdims=True)
    chip_x = (route // 2 - x) & 3
    chip = ((route // 8 - z - chip_x) & 3) * 4 + chip_x
    base = (route & 1) * 1024 + chip * (2 * CAP) + core * CAP
    codes[...] = jnp.broadcast_to(base.astype(jnp.float32) + position, codes.shape)

    pl.semaphore_wait(barrier, len(peers))
    swap_tokens = remote(tokens, partner_tokens, pair_s.at[0], pair_r.at[0], partner)
    swap_tokens.start()
    give_up = remote(tokens.at[:, a], below.at[0], give_s.at[0], give_r.at[0], ups)
    give_down = remote(tokens.at[:, b], above.at[0], give_s.at[1], give_r.at[1], downs)
    give_codes = [
        remote(codes, other_codes.at[i], code_s.at[i], code_r.at[i], peer)
        for i, peer in enumerate(code_peers)
    ]
    for g in give_codes:
        g.start()
    give_up.start()
    give_down.start()

    slot = lax.broadcasted_iota(jnp.int32, (slots, tok), 0)
    shift = core * 1024

    def marks(code):
        return jnp.where(slot == code.astype(jnp.int32) - shift, 1.0, 0.0).astype(jnp.bfloat16)

    place[0, :, 0:tok] = marks(codes[0:1, :])
    give_codes[0].wait_recv()
    place[0, :, tok : 2 * tok] = marks(other_codes[0, 0:1, :])
    swap_tokens.wait_recv()

    def zx_refs(kind, dz, dx, n):
        o, s = (4 - dz) % 4, (4 - dx) % 4
        src, dst = pl.ds(3 * dx, n), pl.ds(3 * s, n)
        if kind == 0:
            return outgoing.at[dz, src], rows_in.at[o, 0, dst]
        if kind == 1:
            return outgoing_side.at[0, dz, src], rows_in.at[o, 3, dst, :, a]
        return outgoing_side.at[1, dz, src], rows_in.at[o, 1, dst, :, b]

    def send_zx(kind, dz, dx):
        src, dst = zx_refs(kind, dz, dx, 3)
        k = ((4 - dz) % 4) * 3 + kind
        return remote(src, dst, zx_s.at[k], zx_r.at[k], owner(dz, dx))

    def all_zx(kind, o):
        if o:
            refs = zx_refs(kind, (4 - o) % 4, 0, 12)
        else:
            src = outgoing.at[0, pl.ds(3, 9)] if kind == 0 else outgoing_side.at[kind - 1, 0, pl.ds(3, 9)]
            part = pl.ds(3, 9)
            dst = (
                rows_in.at[0, 0, part]
                if kind == 0
                else rows_in.at[0, 3, part, :, a]
                if kind == 1
                else rows_in.at[0, 1, part, :, b]
            )
            refs = src, dst
        k = o * 3 + kind
        return remote(*refs, zx_s.at[k], zx_r.at[k], owner(0, 1))

    def forward(o, k):
        src, dst, to = (
            (rows_in.at[o, 0, :, :, a], rows_in.at[o, 1, :, :, a], downs),
            (rows_in.at[o, 0, :, :, b], rows_in.at[o, 3, :, :, b], ups),
            (rows_in.at[o, 3, :, :, a], rows_in.at[o, 2, :, :, a], ups),
            (rows_in.at[o, 1, :, :, b], rows_in.at[o, 2, :, :, b], downs),
        )[k]
        return remote(src, dst, fwd_s.at[o * 4 + k], fwd_r.at[o * 4 + k], to)

    def send_sum(o, k):
        src, to = (
            (partials.at[o, 1, :, :, a], ups),
            (partials.at[o, 3, :, :, b], downs),
            (partials.at[o, 2, :, :, a], downs),
            (partials.at[o, 2, :, :, b], ups),
        )[k]
        return remote(src, arrived.at[o, k], sum_s.at[o * 4 + k], sum_r.at[o * 4 + k], to)

    def back_refs(kind, o, dx, n):
        v, s = (4 - o) % 4, (4 - dx) % 4
        src, dst = pl.ds(3 * dx, n), pl.ds(3 * s, n)
        if kind == 0:
            return partials.at[o, 0, src], returned.at[v, dst]
        if kind == 1:
            return partials.at[o, 3, src, :, a], returned_side.at[0, v, dst]
        return partials.at[o, 1, src, :, b], returned_side.at[1, v, dst]

    def send_back(kind, o, dx):
        src, dst = back_refs(kind, o, dx, 3)
        k = ((4 - o) % 4) * 3 + kind
        return remote(src, dst, back_s.at[k], back_r.at[k], owner(o, dx))

    def all_back(kind, v):
        if v:
            refs = back_refs(kind, (4 - v) % 4, 0, 12)
        else:
            part = pl.ds(3, 9)
            refs = (
                (partials.at[0, 0, part], returned.at[0, part])
                if kind == 0
                else (partials.at[0, 3, part, :, a], returned_side.at[0, 0, part])
                if kind == 1
                else (partials.at[0, 1, part, :, b], returned_side.at[1, 0, part])
            )
        k = v * 3 + kind
        return remote(*refs, back_s.at[k], back_r.at[k], owner(0, 1))

    def pick(k, dz, mine, theirs):
        mark = place[k, dz * group : (dz + 1) * group, :]
        got = jnp.dot(mark[:, 0:tok], mine, preferred_element_type=jnp.float32)
        got += jnp.dot(mark[:, tok:], theirs, preferred_element_type=jnp.float32)
        return got.astype(jnp.bfloat16).reshape(group // 8, 8, half)

    def place_own(o):
        dz = (4 - o) % 4

        for cols in (a, b):
            outgoing[dz, :, :, cols] = pick(0, dz, tokens[:, cols], partner_tokens[:, cols])

        for dx in (2, 1, 3, 0):
            if dz or dx:
                send_zx(0, dz, dx).start()
            else:
                rows_in[0, 0, 0:3] = outgoing[0, 0:3]

    def place_side(o):
        dz = (4 - o) % 4

        outgoing_side[0, dz] = pick(1, dz, below[0], below[1])
        outgoing_side[1, dz] = pick(2, dz, above[0], above[1])

        for dx in (2, 1, 3, 0):
            if dz or dx:
                send_zx(1, dz, dx).start()
                send_zx(2, dz, dx).start()
            else:
                rows_in[0, 3, 0:3, :, 0:half] = outgoing_side[0, 0, 0:3]
                rows_in[0, 1, 0:3, :, half:] = outgoing_side[1, 0, 0:3]

    def forward_own(o):
        all_zx(0, o).wait_recv()
        forward(o, 0).start()
        forward(o, 1).start()

    def forward_side(o):
        all_zx(1, o).wait_recv()
        forward(o, 2).start()
        all_zx(2, o).wait_recv()
        forward(o, 3).start()

    def compute(o, middle):
        for k in range(4):
            forward(o, k).wait_recv()
        for k in range(4):
            lhs[k * group : (k + 1) * group, :] = rows_in[o, k].reshape(group, features)

        @pl.loop(0, hidden.shape[1] // 256)
        def _(n):
            cols = pl.ds(pl.multiple_of(n * 256, 256), 256)
            g = jnp.dot(lhs[...], gate[:, cols], preferred_element_type=jnp.float32)
            u = jnp.dot(lhs[...], up[:, cols], preferred_element_type=jnp.float32)
            hidden[:, cols] = (g / (1.0 + jnp.exp(-g)) * u).astype(jnp.bfloat16)

        if middle is not None:
            if middle == ORDER[2]:
                forward_own(ORDER[3])
            forward_side(middle)

        @pl.loop(0, features // 256)
        def _(n):
            cols = pl.ds(pl.multiple_of(n * 256, 256), 256)
            p = jnp.dot(hidden[...], down[:, cols], preferred_element_type=jnp.float32)
            partials[o, :, :, :, cols] = p.astype(jnp.bfloat16).reshape(4, group // 8, 8, 256)

        for k in (2, 3, 0, 1):
            send_sum(o, k).start()

    def added(o, k, part, cols, addends):
        total = partials[o, k, part, :, cols].astype(jnp.float32)
        for addend in addends:
            total += addend[part].astype(jnp.float32)
        return total.astype(jnp.bfloat16)

    def finish(o):
        for which in range(4):
            send_sum(o, which).wait_recv()
        for dx in (2, 1, 3, 0):
            part = pl.ds(3 * dx, 3)
            partials[o, 3, part, :, a] = added(o, 3, part, a, [arrived.at[o, 2]])
            partials[o, 1, part, :, b] = added(o, 1, part, b, [arrived.at[o, 3]])
            partials[o, 0, part, :, a] = added(o, 0, part, a, [arrived.at[o, 0]])
            partials[o, 0, part, :, b] = added(o, 0, part, b, [arrived.at[o, 1]])
            if o or dx:
                for kind in (1, 2, 0):
                    send_back(kind, o, dx).start()
            else:
                returned[0, 0:3] = partials[0, 0, 0:3]
                returned_side[0, 0, 0:3] = partials[0, 3, 0:3, :, 0:half]
                returned_side[1, 0, 0:3] = partials[0, 1, 0:3, :, half:]

    last = ORDER[3]
    unused = (4 - last) % 4
    pass_down = remote(partials.at[last, 3, :, :, a], passed.at[0], pass_s.at[0], pass_r.at[0], downs)
    pass_up = remote(partials.at[last, 1, :, :, b], passed.at[1], pass_s.at[1], pass_r.at[1], ups)

    def pass_sums():
        everything = pl.ds(0, group // 8)
        send_sum(last, 2).wait_recv()
        partials[last, 3, :, :, a] = added(last, 3, everything, a, [arrived.at[last, 2]])
        pass_down.start()
        send_sum(last, 3).wait_recv()
        partials[last, 1, :, :, b] = added(last, 1, everything, b, [arrived.at[last, 3]])
        pass_up.start()

    def finish_last():
        send_sum(last, 0).wait_recv()
        send_sum(last, 1).wait_recv()
        pass_down.wait_recv()
        pass_up.wait_recv()
        for dx in (2, 1, 3, 0):
            part = pl.ds(3 * dx, 3)
            partials[last, 0, part, :, a] = added(last, 0, part, a, [arrived.at[last, 0], passed.at[0]])
            partials[last, 0, part, :, b] = added(last, 0, part, b, [arrived.at[last, 1], passed.at[1]])
            send_back(0, last, dx).start()

    place_own(ORDER[0])
    place_own(ORDER[1])
    for i, (k, c) in enumerate(((1, 0), (1, 1), (2, 0), (2, 1))):
        give_codes[i + 1].wait_recv()
        place[k, :, c * tok : (c + 1) * tok] = marks(other_codes[i + 1, 0:1, :])
    forward_own(ORDER[0])
    give_up.wait_recv()
    swap_below = remote(below.at[0], below.at[1], pair_s.at[2], pair_r.at[2], partner)
    swap_below.start()
    give_down.wait_recv()
    swap_above = remote(above.at[0], above.at[1], pair_s.at[3], pair_r.at[3], partner)
    swap_above.start()
    place_own(ORDER[2])
    swap_below.wait_recv()
    swap_above.wait_recv()
    place_side(ORDER[0])
    place_side(ORDER[1])
    forward_own(ORDER[1])
    place_own(ORDER[3])
    forward_side(ORDER[0])
    place_side(ORDER[2])
    place_side(ORDER[3])
    for w in weights:
        w.wait()
    for i, o in enumerate(ORDER):
        if i == 0:
            forward_own(ORDER[2])
            forward_side(ORDER[1])
        compute(o, ORDER[i + 2] if i + 2 < 4 else None)
        if i >= 1:
            finish(ORDER[i - 1])
    pass_sums()

    slot_lane = lax.broadcasted_iota(jnp.int32, (tok, slots), 1)

    def picks(code_row):
        code = jnp.broadcast_to(code_row, (tok, tok)).T[:, 0:1].astype(jnp.int32)
        return jnp.where(slot_lane == code - shift, 1.0, 0.0).astype(jnp.bfloat16)

    def picked(code_row, source):
        return jnp.dot(picks(code_row), source, preferred_element_type=jnp.float32)

    def picked_last(code_row, source):
        return jnp.dot(
            picks(code_row)[:, unused * group : (unused + 1) * group], source, preferred_element_type=jnp.float32
        )

    for o in ORDER[:3]:
        all_back(1, (4 - o) % 4).wait_recv()
        all_back(2, (4 - o) % 4).wait_recv()
    returned_side[:, unused] = jnp.zeros((2, group // 8, 8, half), jnp.bfloat16)
    for v in range(4):
        rows = slice(v * group, (v + 1) * group)
        lhs[rows, 0:half] = returned_side[0, v].reshape(group, half)
        lhs[rows, half:] = returned_side[1, v].reshape(group, half)
    side_out[0] = picked(other_codes[2, 0:1, :], lhs[:, 0:half]).astype(jnp.bfloat16)
    swap_side_a = remote(side_out.at[0], side_in.at[0], pair_s.at[4], pair_r.at[4], partner)
    swap_side_a.start()
    side_out[1] = picked(other_codes[4, 0:1, :], lhs[:, half:]).astype(jnp.bfloat16)
    swap_side_b = remote(side_out.at[1], side_in.at[1], pair_s.at[5], pair_r.at[5], partner)
    swap_side_b.start()
    mine_a = picked(other_codes[1, 0:1, :], lhs[:, 0:half])
    swap_side_a.wait_recv()
    sides[0] = (mine_a + side_in[0].astype(jnp.float32)).astype(jnp.bfloat16)
    home_down = remote(sides.at[0], home.at[0], home_s.at[0], home_r.at[0], downs)
    home_down.start()
    mine_b = picked(other_codes[3, 0:1, :], lhs[:, half:])
    swap_side_b.wait_recv()
    sides[1] = (mine_b + side_in[1].astype(jnp.float32)).astype(jnp.bfloat16)
    home_up = remote(sides.at[1], home.at[1], home_s.at[1], home_r.at[1], ups)
    home_up.start()
    for o in ORDER[:3]:
        all_back(0, (4 - o) % 4).wait_recv()
    for v in range(4):
        rows = slice(v * group, (v + 1) * group)
        lhs[rows, :] = jnp.zeros((group, features), lhs.dtype) if v == unused else returned[v].reshape(group, features)
    theirs = picked(other_codes[0, 0:1, :], lhs[...])
    mine = picked(codes[0:1, :], lhs[...])
    finish_last()
    all_back(0, unused).wait_recv()
    lhs[0:group, :] = returned[unused].reshape(group, features)
    theirs += picked_last(other_codes[0, 0:1, :], lhs[0:group, :])
    cross_out[...] = theirs.astype(jnp.bfloat16)
    swap_back = remote(cross_out, cross_in, pair_s.at[1], pair_r.at[1], partner)
    swap_back.start()
    mine += picked_last(codes[0:1, :], lhs[0:group, :])
    score = jnp.broadcast_to(scores[...], (tok, tok)).T[:, 0:1]
    swap_back.wait_recv()
    home_down.wait_recv()
    out[:, 0:half] = (
        score * (mine[:, 0:half] + cross_in[:, 0:half].astype(jnp.float32) + home[0].astype(jnp.float32))
    ).astype(jnp.bfloat16)
    home_up.wait_recv()
    out[:, half:] = (
        score * (mine[:, half:] + cross_in[:, half:].astype(jnp.float32) + home[1].astype(jnp.float32))
    ).astype(jnp.bfloat16)

    for c in (
        swap_tokens,
        give_up,
        give_down,
        swap_below,
        swap_above,
        swap_side_a,
        swap_side_b,
        home_down,
        home_up,
        swap_back,
        pass_down,
        pass_up,
        *give_codes,
    ):
        c.wait_send()
    for o in range(4):
        for kind in range(3):
            all_zx(kind, o).wait_send()
            if kind == 0 or o != unused:
                all_back(kind, o).wait_send()
        for k in range(4):
            forward(o, k).wait_send()
            send_sum(o, k).wait_send()


def local(tokens, routes, scores, gate_weight, up_weight, down_weight):
    tok, features = tokens.shape
    hid = gate_weight.shape[2]
    half = features // 2
    slots = 32 * CAP
    group = slots // 4
    g8 = group // 8
    bf = jnp.bfloat16
    vmem = pl.BlockSpec(memory_space=pltpu.VMEM)
    hbm = pl.BlockSpec(memory_space=pl.ANY)
    sizes = (
        (features, hid),
        (features, hid),
        (hid, features),
        None,
        None,
        (tok, features),
        (2, tok, half),
        (2, tok, half),
        (3, slots, 2 * tok),
        (4, g8, 8, features),
        (2, 4, g8, 8, half),
        (4, 4, g8, 8, features),
        (slots, features),
        (slots, hid),
        (4, 4, g8, 8, features),
        (4, 4, g8, 8, half),
        (4, g8, 8, features),
        (2, 4, g8, 8, half),
        (tok, features),
        (tok, features),
        (2, tok, half),
        (2, tok, half),
        (2, tok, half),
        (2, tok, half),
        (2, g8, 8, half),
    )
    scratch = [pltpu.VMEM(s, bf) if s else None for s in sizes]
    scratch[3] = pltpu.VMEM((8, tok), jnp.float32)
    scratch[4] = pltpu.VMEM((5, 8, tok), jnp.float32)
    counts = (3, 6, 6, 5, 5, 2, 2, 12, 12, 16, 16, 16, 16, 12, 12, 2, 2, 2, 2)
    return pl.pallas_call(
        layer,
        out_shape=jax.ShapeDtypeStruct((tok, features), bf),
        in_specs=[vmem] * 3 + [hbm] * 3,
        out_specs=vmem,
        scratch_shapes=scratch + [pltpu.SemaphoreType.DMA((n,)) for n in counts],
        compiler_params=pltpu.CompilerParams(
            collective_id=0, has_side_effects=True, vmem_limit_bytes=62 * 1024 * 1024
        ),
    )(
        tokens,
        routes.reshape(1, tok),
        scores.reshape(1, tok),
        gate_weight[0],
        up_weight[0],
        down_weight[0],
    )


def solution(mesh):
    in_specs = (
        P(("expert", "etp"), None),
        P(("expert", "etp"), None),
        P(("expert", "etp")),
        P("expert", None, "etp"),
        P("expert", None, "etp"),
        P("expert", "etp", None),
    )
    out_specs = P(("expert", "etp"), None)
    return jax.shard_map(local, mesh=mesh, in_specs=in_specs, out_specs=out_specs, check_vma=False)
```

```python
import jax
import jax.numpy as jnp
from jax import lax
from jax.experimental import pallas as pl
from jax.experimental.pallas import tpu as pltpu
from jax.sharding import PartitionSpec as P

MESH = pl.DeviceIdType.MESH
CAP = 12
ORDER = (0, 1, 3, 2)


def layer(
    tokens,
    routes,
    scores,
    gate_hbm,
    up_hbm,
    down_hbm,
    out,
    gate,
    up,
    down,
    codes,
    other_codes,
    partner_tokens,
    below,
    above,
    place,
    outgoing,
    outgoing_side,
    rows_in,
    lhs,
    hidden,
    partials,
    arrived,
    returned,
    returned_side,
    cross_out,
    cross_in,
    side_out,
    side_in,
    sides,
    home,
    passed,
    weight_sem,
    pair_s,
    pair_r,
    code_s,
    code_r,
    give_s,
    give_r,
    zx_s,
    zx_r,
    fwd_s,
    fwd_r,
    sum_s,
    sum_r,
    back_s,
    back_r,
    home_s,
    home_r,
    pass_s,
    pass_r,
):
    e, y = lax.axis_index("expert"), lax.axis_index("etp")
    core, x, z = e % 2, (e // 2) % 4, e // 8
    tok, features = tokens.shape
    half = features // 2
    a, b = pl.ds(0, half), pl.ds(half, half)
    slots = place.shape[1]
    group = slots // 4
    pe = e + 1 - 2 * core
    y_up, y_down = (y + 1) % 4, (y + 3) % 4
    partner, ups, downs = (pe, y), (e, y_up), (e, y_down)

    def owner(dz, dx):
        return ((((z + dz + dx) % 4) * 4 + (x + dx) % 4) * 2 + core, y)

    def remote(src, dst, send, recv, to):
        return pltpu.make_async_remote_copy(
            src_ref=src, dst_ref=dst, send_sem=send, recv_sem=recv, device_id=to, device_id_type=MESH
        )

    weights = [
        pltpu.make_async_copy(gate_hbm, gate, weight_sem.at[0]),
        pltpu.make_async_copy(up_hbm, up, weight_sem.at[1]),
        pltpu.make_async_copy(down_hbm, down, weight_sem.at[2]),
    ]
    code_peers = (partner, ups, (pe, y_up), downs, (pe, y_down))
    barrier = pltpu.get_barrier_semaphore()
    peers = [owner(dz, dx) for dz in range(4) for dx in range(4) if dz or dx] + list(code_peers)
    for peer in peers:
        pl.semaphore_signal(barrier, inc=1, device_id=peer, device_id_type=MESH)
    for w in weights:
        w.start()

    first = lax.broadcasted_iota(jnp.int32, (tok, tok), 0)
    second = lax.broadcasted_iota(jnp.int32, (tok, tok), 1)
    route = routes[...]
    route_rows = jnp.broadcast_to(route.astype(jnp.float32), (tok, tok))
    same = route_rows == route_rows.T
    position = jnp.sum(jnp.where(same & (first < second), 1.0, 0.0), axis=0, keepdims=True)
    chip_x = (route // 2 - x) & 3
    chip = ((route // 8 - z - chip_x) & 3) * 4 + chip_x
    base = (route & 1) * 1024 + chip * (2 * CAP) + core * CAP
    codes[...] = jnp.broadcast_to(base.astype(jnp.float32) + position, codes.shape)

    pl.semaphore_wait(barrier, len(peers))
    swap_tokens = remote(tokens, partner_tokens, pair_s.at[0], pair_r.at[0], partner)
    swap_tokens.start()
    give_up = remote(tokens.at[:, a], below.at[0], give_s.at[0], give_r.at[0], ups)
    give_down = remote(tokens.at[:, b], above.at[0], give_s.at[1], give_r.at[1], downs)
    give_codes = [
        remote(codes, other_codes.at[i], code_s.at[i], code_r.at[i], peer)
        for i, peer in enumerate(code_peers)
    ]
    for g in give_codes:
        g.start()
    give_up.start()
    give_down.start()

    slot = lax.broadcasted_iota(jnp.int32, (slots, tok), 0)
    shift = core * 1024

    def marks(code):
        return jnp.where(slot == code.astype(jnp.int32) - shift, 1.0, 0.0).astype(jnp.bfloat16)

    place[0, :, 0:tok] = marks(codes[0:1, :])
    give_codes[0].wait_recv()
    place[0, :, tok : 2 * tok] = marks(other_codes[0, 0:1, :])
    swap_tokens.wait_recv()

    def zx_refs(kind, dz, dx, n):
        o, s = (4 - dz) % 4, (4 - dx) % 4
        src, dst = pl.ds(3 * dx, n), pl.ds(3 * s, n)
        if kind == 0:
            return outgoing.at[dz, src], rows_in.at[o, 0, dst]
        if kind == 1:
            return outgoing_side.at[0, dz, src], rows_in.at[o, 3, dst, :, a]
        return outgoing_side.at[1, dz, src], rows_in.at[o, 1, dst, :, b]

    def send_zx(kind, dz, dx):
        src, dst = zx_refs(kind, dz, dx, 3)
        k = ((4 - dz) % 4) * 3 + kind
        return remote(src, dst, zx_s.at[k], zx_r.at[k], owner(dz, dx))

    def all_zx(kind, o):
        if o:
            refs = zx_refs(kind, (4 - o) % 4, 0, 12)
        else:
            src = outgoing.at[0, pl.ds(3, 9)] if kind == 0 else outgoing_side.at[kind - 1, 0, pl.ds(3, 9)]
            part = pl.ds(3, 9)
            dst = (
                rows_in.at[0, 0, part]
                if kind == 0
                else rows_in.at[0, 3, part, :, a]
                if kind == 1
                else rows_in.at[0, 1, part, :, b]
            )
            refs = src, dst
        k = o * 3 + kind
        return remote(*refs, zx_s.at[k], zx_r.at[k], owner(0, 1))

    def forward(o, k):
        src, dst, to = (
            (rows_in.at[o, 0, :, :, a], rows_in.at[o, 1, :, :, a], downs),
            (rows_in.at[o, 0, :, :, b], rows_in.at[o, 3, :, :, b], ups),
            (rows_in.at[o, 3, :, :, a], rows_in.at[o, 2, :, :, a], ups),
            (rows_in.at[o, 1, :, :, b], rows_in.at[o, 2, :, :, b], downs),
        )[k]
        return remote(src, dst, fwd_s.at[o * 4 + k], fwd_r.at[o * 4 + k], to)

    def send_sum(o, k):
        src, to = (
            (partials.at[o, 1, :, :, a], ups),
            (partials.at[o, 3, :, :, b], downs),
            (partials.at[o, 2, :, :, a], downs),
            (partials.at[o, 2, :, :, b], ups),
        )[k]
        return remote(src, arrived.at[o, k], sum_s.at[o * 4 + k], sum_r.at[o * 4 + k], to)

    def back_refs(kind, o, dx, n):
        v, s = (4 - o) % 4, (4 - dx) % 4
        src, dst = pl.ds(3 * dx, n), pl.ds(3 * s, n)
        if kind == 0:
            return partials.at[o, 0, src], returned.at[v, dst]
        if kind == 1:
            return partials.at[o, 3, src, :, a], returned_side.at[0, v, dst]
        return partials.at[o, 1, src, :, b], returned_side.at[1, v, dst]

    def send_back(kind, o, dx):
        src, dst = back_refs(kind, o, dx, 3)
        k = ((4 - o) % 4) * 3 + kind
        return remote(src, dst, back_s.at[k], back_r.at[k], owner(o, dx))

    def all_back(kind, v):
        if v:
            refs = back_refs(kind, (4 - v) % 4, 0, 12)
        else:
            part = pl.ds(3, 9)
            refs = (
                (partials.at[0, 0, part], returned.at[0, part])
                if kind == 0
                else (partials.at[0, 3, part, :, a], returned_side.at[0, 0, part])
                if kind == 1
                else (partials.at[0, 1, part, :, b], returned_side.at[1, 0, part])
            )
        k = v * 3 + kind
        return remote(*refs, back_s.at[k], back_r.at[k], owner(0, 1))

    def pick(k, dz, mine, theirs):
        mark = place[k, dz * group : (dz + 1) * group, :]
        got = jnp.dot(mark[:, 0:tok], mine, preferred_element_type=jnp.float32)
        got += jnp.dot(mark[:, tok:], theirs, preferred_element_type=jnp.float32)
        return got.astype(jnp.bfloat16).reshape(group // 8, 8, half)

    def place_own(o):
        dz = (4 - o) % 4

        for cols in (a, b):
            outgoing[dz, :, :, cols] = pick(0, dz, tokens[:, cols], partner_tokens[:, cols])

        for dx in (2, 1, 3, 0):
            if dz or dx:
                send_zx(0, dz, dx).start()
            else:
                rows_in[0, 0, 0:3] = outgoing[0, 0:3]

    def place_side(o):
        dz = (4 - o) % 4

        outgoing_side[0, dz] = pick(1, dz, below[0], below[1])
        outgoing_side[1, dz] = pick(2, dz, above[0], above[1])

        for dx in (2, 1, 3, 0):
            if dz or dx:
                send_zx(1, dz, dx).start()
                send_zx(2, dz, dx).start()
            else:
                rows_in[0, 3, 0:3, :, 0:half] = outgoing_side[0, 0, 0:3]
                rows_in[0, 1, 0:3, :, half:] = outgoing_side[1, 0, 0:3]

    def forward_own(o):
        all_zx(0, o).wait_recv()
        forward(o, 0).start()
        forward(o, 1).start()

    def forward_side(o):
        all_zx(1, o).wait_recv()
        forward(o, 2).start()
        all_zx(2, o).wait_recv()
        forward(o, 3).start()

    def compute(o, middle):
        for k in range(4):
            forward(o, k).wait_recv()
        for k in range(4):
            lhs[k * group : (k + 1) * group, :] = rows_in[o, k].reshape(group, features)

        @pl.loop(0, hidden.shape[1] // 256)
        def _(n):
            cols = pl.ds(pl.multiple_of(n * 256, 256), 256)
            g = jnp.dot(lhs[...], gate[:, cols], preferred_element_type=jnp.float32)
            u = jnp.dot(lhs[...], up[:, cols], preferred_element_type=jnp.float32)
            hidden[:, cols] = (g / (1.0 + jnp.exp(-g)) * u).astype(jnp.bfloat16)

        if middle is not None:
            if middle == ORDER[2]:
                forward_own(ORDER[3])
            forward_side(middle)

        for side in (0, 1):

            @pl.loop(side * half // 256, (side + 1) * half // 256)
            def _(n):
                cols = pl.ds(pl.multiple_of(n * 256, 256), 256)
                p = jnp.dot(hidden[...], down[:, cols], preferred_element_type=jnp.float32)
                partials[o, :, :, :, cols] = p.astype(jnp.bfloat16).reshape(4, group // 8, 8, 256)

            send_sum(o, 2 + side).start()
            send_sum(o, side).start()

    def added(o, k, part, cols, addends):
        total = partials[o, k, part, :, cols].astype(jnp.float32)
        for addend in addends:
            total += addend[part].astype(jnp.float32)
        return total.astype(jnp.bfloat16)

    def finish(o):
        for which in range(4):
            send_sum(o, which).wait_recv()
        for dx in (2, 1, 3, 0):
            part = pl.ds(3 * dx, 3)
            partials[o, 3, part, :, a] = added(o, 3, part, a, [arrived.at[o, 2]])
            partials[o, 1, part, :, b] = added(o, 1, part, b, [arrived.at[o, 3]])
            partials[o, 0, part, :, a] = added(o, 0, part, a, [arrived.at[o, 0]])
            partials[o, 0, part, :, b] = added(o, 0, part, b, [arrived.at[o, 1]])
            if o or dx:
                for kind in (1, 2, 0):
                    send_back(kind, o, dx).start()
            else:
                returned[0, 0:3] = partials[0, 0, 0:3]
                returned_side[0, 0, 0:3] = partials[0, 3, 0:3, :, 0:half]
                returned_side[1, 0, 0:3] = partials[0, 1, 0:3, :, half:]

    last = ORDER[3]
    unused = (4 - last) % 4
    pass_down = remote(partials.at[last, 3, :, :, a], passed.at[0], pass_s.at[0], pass_r.at[0], downs)
    pass_up = remote(partials.at[last, 1, :, :, b], passed.at[1], pass_s.at[1], pass_r.at[1], ups)

    def pass_sums():
        everything = pl.ds(0, group // 8)
        send_sum(last, 2).wait_recv()
        partials[last, 3, :, :, a] = added(last, 3, everything, a, [arrived.at[last, 2]])
        pass_down.start()
        send_sum(last, 3).wait_recv()
        partials[last, 1, :, :, b] = added(last, 1, everything, b, [arrived.at[last, 3]])
        pass_up.start()

    def finish_last():
        send_sum(last, 0).wait_recv()
        send_sum(last, 1).wait_recv()
        pass_down.wait_recv()
        pass_up.wait_recv()
        for dx in (2, 1, 3, 0):
            part = pl.ds(3 * dx, 3)
            partials[last, 0, part, :, a] = added(last, 0, part, a, [arrived.at[last, 0], passed.at[0]])
            partials[last, 0, part, :, b] = added(last, 0, part, b, [arrived.at[last, 1], passed.at[1]])
            send_back(0, last, dx).start()

    place_own(ORDER[0])
    place_own(ORDER[1])
    for i, (k, c) in enumerate(((1, 0), (1, 1), (2, 0), (2, 1))):
        give_codes[i + 1].wait_recv()
        place[k, :, c * tok : (c + 1) * tok] = marks(other_codes[i + 1, 0:1, :])
    forward_own(ORDER[0])
    give_up.wait_recv()
    swap_below = remote(below.at[0], below.at[1], pair_s.at[2], pair_r.at[2], partner)
    swap_below.start()
    give_down.wait_recv()
    swap_above = remote(above.at[0], above.at[1], pair_s.at[3], pair_r.at[3], partner)
    swap_above.start()
    place_own(ORDER[2])
    swap_below.wait_recv()
    swap_above.wait_recv()
    place_side(ORDER[0])
    place_side(ORDER[1])
    forward_own(ORDER[1])
    place_own(ORDER[3])
    forward_side(ORDER[0])
    place_side(ORDER[2])
    place_side(ORDER[3])
    for w in weights:
        w.wait()
    for i, o in enumerate(ORDER):
        if i == 0:
            forward_own(ORDER[2])
            forward_side(ORDER[1])
        compute(o, ORDER[i + 2] if i + 2 < 4 else None)
        if i >= 2:
            finish(ORDER[i - 2])
    finish(ORDER[2])
    pass_sums()

    slot_lane = lax.broadcasted_iota(jnp.int32, (tok, slots), 1)

    def picks(code_row):
        code = jnp.broadcast_to(code_row, (tok, tok)).T[:, 0:1].astype(jnp.int32)
        return jnp.where(slot_lane == code - shift, 1.0, 0.0).astype(jnp.bfloat16)

    def picked(code_row, source):
        return jnp.dot(picks(code_row), source, preferred_element_type=jnp.float32)

    def picked_last(code_row, source):
        return jnp.dot(
            picks(code_row)[:, unused * group : (unused + 1) * group], source, preferred_element_type=jnp.float32
        )

    for o in ORDER[:3]:
        all_back(1, (4 - o) % 4).wait_recv()
        all_back(2, (4 - o) % 4).wait_recv()
    returned_side[:, unused] = jnp.zeros((2, group // 8, 8, half), jnp.bfloat16)
    for v in range(4):
        rows = slice(v * group, (v + 1) * group)
        lhs[rows, 0:half] = returned_side[0, v].reshape(group, half)
        lhs[rows, half:] = returned_side[1, v].reshape(group, half)
    side_out[0] = picked(other_codes[2, 0:1, :], lhs[:, 0:half]).astype(jnp.bfloat16)
    swap_side_a = remote(side_out.at[0], side_in.at[0], pair_s.at[4], pair_r.at[4], partner)
    swap_side_a.start()
    side_out[1] = picked(other_codes[4, 0:1, :], lhs[:, half:]).astype(jnp.bfloat16)
    swap_side_b = remote(side_out.at[1], side_in.at[1], pair_s.at[5], pair_r.at[5], partner)
    swap_side_b.start()
    mine_a = picked(other_codes[1, 0:1, :], lhs[:, 0:half])
    swap_side_a.wait_recv()
    sides[0] = (mine_a + side_in[0].astype(jnp.float32)).astype(jnp.bfloat16)
    home_down = remote(sides.at[0], home.at[0], home_s.at[0], home_r.at[0], downs)
    home_down.start()
    mine_b = picked(other_codes[3, 0:1, :], lhs[:, half:])
    swap_side_b.wait_recv()
    sides[1] = (mine_b + side_in[1].astype(jnp.float32)).astype(jnp.bfloat16)
    home_up = remote(sides.at[1], home.at[1], home_s.at[1], home_r.at[1], ups)
    home_up.start()
    for o in ORDER[:3]:
        all_back(0, (4 - o) % 4).wait_recv()
    for v in range(4):
        rows = slice(v * group, (v + 1) * group)
        lhs[rows, :] = jnp.zeros((group, features), lhs.dtype) if v == unused else returned[v].reshape(group, features)
    theirs = picked(other_codes[0, 0:1, :], lhs[...])
    mine = picked(codes[0:1, :], lhs[...])
    finish_last()
    all_back(0, unused).wait_recv()
    lhs[0:group, :] = returned[unused].reshape(group, features)
    theirs += picked_last(other_codes[0, 0:1, :], lhs[0:group, :])
    cross_out[...] = theirs.astype(jnp.bfloat16)
    swap_back = remote(cross_out, cross_in, pair_s.at[1], pair_r.at[1], partner)
    swap_back.start()
    mine += picked_last(codes[0:1, :], lhs[0:group, :])
    score = jnp.broadcast_to(scores[...], (tok, tok)).T[:, 0:1]
    swap_back.wait_recv()
    home_down.wait_recv()
    out[:, 0:half] = (
        score * (mine[:, 0:half] + cross_in[:, 0:half].astype(jnp.float32) + home[0].astype(jnp.float32))
    ).astype(jnp.bfloat16)
    home_up.wait_recv()
    out[:, half:] = (
        score * (mine[:, half:] + cross_in[:, half:].astype(jnp.float32) + home[1].astype(jnp.float32))
    ).astype(jnp.bfloat16)

    for c in (
        swap_tokens,
        give_up,
        give_down,
        swap_below,
        swap_above,
        swap_side_a,
        swap_side_b,
        home_down,
        home_up,
        swap_back,
        pass_down,
        pass_up,
        *give_codes,
    ):
        c.wait_send()
    for o in range(4):
        for kind in range(3):
            all_zx(kind, o).wait_send()
            if kind == 0 or o != unused:
                all_back(kind, o).wait_send()
        for k in range(4):
            forward(o, k).wait_send()
            send_sum(o, k).wait_send()


def local(tokens, routes, scores, gate_weight, up_weight, down_weight):
    tok, features = tokens.shape
    hid = gate_weight.shape[2]
    half = features // 2
    slots = 32 * CAP
    group = slots // 4
    g8 = group // 8
    bf = jnp.bfloat16
    vmem = pl.BlockSpec(memory_space=pltpu.VMEM)
    hbm = pl.BlockSpec(memory_space=pl.ANY)
    sizes = (
        (features, hid),
        (features, hid),
        (hid, features),
        None,
        None,
        (tok, features),
        (2, tok, half),
        (2, tok, half),
        (3, slots, 2 * tok),
        (4, g8, 8, features),
        (2, 4, g8, 8, half),
        (4, 4, g8, 8, features),
        (slots, features),
        (slots, hid),
        (4, 4, g8, 8, features),
        (4, 4, g8, 8, half),
        (4, g8, 8, features),
        (2, 4, g8, 8, half),
        (tok, features),
        (tok, features),
        (2, tok, half),
        (2, tok, half),
        (2, tok, half),
        (2, tok, half),
        (2, g8, 8, half),
    )
    scratch = [pltpu.VMEM(s, bf) if s else None for s in sizes]
    scratch[3] = pltpu.VMEM((8, tok), jnp.float32)
    scratch[4] = pltpu.VMEM((5, 8, tok), jnp.float32)
    counts = (3, 6, 6, 5, 5, 2, 2, 12, 12, 16, 16, 16, 16, 12, 12, 2, 2, 2, 2)
    return pl.pallas_call(
        layer,
        out_shape=jax.ShapeDtypeStruct((tok, features), bf),
        in_specs=[vmem] * 3 + [hbm] * 3,
        out_specs=vmem,
        scratch_shapes=scratch + [pltpu.SemaphoreType.DMA((n,)) for n in counts],
        compiler_params=pltpu.CompilerParams(
            collective_id=0, has_side_effects=True, vmem_limit_bytes=62 * 1024 * 1024
        ),
    )(
        tokens,
        routes.reshape(1, tok),
        scores.reshape(1, tok),
        gate_weight[0],
        up_weight[0],
        down_weight[0],
    )


def solution(mesh):
    in_specs = (
        P(("expert", "etp"), None),
        P(("expert", "etp"), None),
        P(("expert", "etp")),
        P("expert", None, "etp"),
        P("expert", None, "etp"),
        P("expert", "etp", None),
    )
    out_specs = P(("expert", "etp"), None)
    return jax.shard_map(local, mesh=mesh, in_specs=in_specs, out_specs=out_specs, check_vma=False)
```

```python
import jax
import jax.numpy as jnp
from jax import lax
from jax.experimental import pallas as pl
from jax.experimental.pallas import tpu as pltpu
from jax.sharding import PartitionSpec as P

MESH = pl.DeviceIdType.MESH
CAP = 12
ORDER = (0, 1, 3, 2)


def layer(
    tokens,
    routes,
    scores,
    gate_hbm,
    up_hbm,
    down_hbm,
    out,
    gate,
    up,
    down,
    codes,
    other_codes,
    partner_tokens,
    below,
    above,
    place,
    outgoing,
    outgoing_side,
    rows_in,
    lhs,
    hidden,
    partials,
    arrived,
    returned,
    returned_side,
    cross_out,
    cross_in,
    side_out,
    side_in,
    sides,
    home,
    passed,
    weight_sem,
    pair_s,
    pair_r,
    code_s,
    code_r,
    give_s,
    give_r,
    zx_s,
    zx_r,
    fwd_s,
    fwd_r,
    sum_s,
    sum_r,
    back_s,
    back_r,
    home_s,
    home_r,
    pass_s,
    pass_r,
):
    e, y = lax.axis_index("expert"), lax.axis_index("etp")
    core, x, z = e % 2, (e // 2) % 4, e // 8
    tok, features = tokens.shape
    half = features // 2
    a, b = pl.ds(0, half), pl.ds(half, half)
    slots = place.shape[1]
    group = slots // 4
    pe = e + 1 - 2 * core
    y_up, y_down = (y + 1) % 4, (y + 3) % 4
    partner, ups, downs = (pe, y), (e, y_up), (e, y_down)

    def owner(dz, dx):
        return ((((z + dz + dx) % 4) * 4 + (x + dx) % 4) * 2 + core, y)

    def remote(src, dst, send, recv, to):
        return pltpu.make_async_remote_copy(
            src_ref=src, dst_ref=dst, send_sem=send, recv_sem=recv, device_id=to, device_id_type=MESH
        )

    weights = [
        pltpu.make_async_copy(gate_hbm, gate, weight_sem.at[0]),
        pltpu.make_async_copy(up_hbm, up, weight_sem.at[1]),
        pltpu.make_async_copy(down_hbm, down, weight_sem.at[2]),
    ]
    code_peers = (partner, ups, (pe, y_up), downs, (pe, y_down))
    barrier = pltpu.get_barrier_semaphore()
    peers = [owner(dz, dx) for dz in range(4) for dx in range(4) if dz or dx] + list(code_peers)
    for peer in peers:
        pl.semaphore_signal(barrier, inc=1, device_id=peer, device_id_type=MESH)
    for w in weights:
        w.start()

    first = lax.broadcasted_iota(jnp.int32, (tok, tok), 0)
    second = lax.broadcasted_iota(jnp.int32, (tok, tok), 1)
    route = routes[...]
    route_rows = jnp.broadcast_to(route.astype(jnp.float32), (tok, tok))
    same = route_rows == route_rows.T
    position = jnp.sum(jnp.where(same & (first < second), 1.0, 0.0), axis=0, keepdims=True)
    chip_x = (route // 2 - x) & 3
    chip = ((route // 8 - z - chip_x) & 3) * 4 + chip_x
    base = (route & 1) * 1024 + chip * (2 * CAP) + core * CAP
    codes[...] = jnp.broadcast_to(base.astype(jnp.float32) + position, codes.shape)

    pl.semaphore_wait(barrier, len(peers))
    swap_tokens = remote(tokens, partner_tokens, pair_s.at[0], pair_r.at[0], partner)
    swap_tokens.start()
    give_up = remote(tokens.at[:, a], below.at[0], give_s.at[0], give_r.at[0], ups)
    give_down = remote(tokens.at[:, b], above.at[0], give_s.at[1], give_r.at[1], downs)
    give_codes = [
        remote(codes, other_codes.at[i], code_s.at[i], code_r.at[i], peer)
        for i, peer in enumerate(code_peers)
    ]
    give_up.start()
    give_down.start()
    for g in give_codes:
        g.start()

    slot = lax.broadcasted_iota(jnp.int32, (slots, tok), 0)
    shift = core * 1024

    def marks(code):
        return jnp.where(slot == code.astype(jnp.int32) - shift, 1.0, 0.0).astype(jnp.bfloat16)

    place[0, :, 0:tok] = marks(codes[0:1, :])
    give_codes[0].wait_recv()
    place[0, :, tok : 2 * tok] = marks(other_codes[0, 0:1, :])
    swap_tokens.wait_recv()

    def zx_refs(kind, dz, dx, n):
        o, s = (4 - dz) % 4, (4 - dx) % 4
        src, dst = pl.ds(3 * dx, n), pl.ds(3 * s, n)
        if kind == 0:
            return outgoing.at[dz, src], rows_in.at[o, 0, dst]
        if kind == 1:
            return outgoing_side.at[0, dz, src], rows_in.at[o, 3, dst, :, a]
        return outgoing_side.at[1, dz, src], rows_in.at[o, 1, dst, :, b]

    def send_zx(kind, dz, dx):
        src, dst = zx_refs(kind, dz, dx, 3)
        k = ((4 - dz) % 4) * 3 + kind
        return remote(src, dst, zx_s.at[k], zx_r.at[k], owner(dz, dx))

    def all_zx(kind, o):
        if o:
            refs = zx_refs(kind, (4 - o) % 4, 0, 12)
        else:
            src = outgoing.at[0, pl.ds(3, 9)] if kind == 0 else outgoing_side.at[kind - 1, 0, pl.ds(3, 9)]
            part = pl.ds(3, 9)
            dst = (
                rows_in.at[0, 0, part]
                if kind == 0
                else rows_in.at[0, 3, part, :, a]
                if kind == 1
                else rows_in.at[0, 1, part, :, b]
            )
            refs = src, dst
        k = o * 3 + kind
        return remote(*refs, zx_s.at[k], zx_r.at[k], owner(0, 1))

    def forward(o, k):
        src, dst, to = (
            (rows_in.at[o, 0, :, :, a], rows_in.at[o, 1, :, :, a], downs),
            (rows_in.at[o, 0, :, :, b], rows_in.at[o, 3, :, :, b], ups),
            (rows_in.at[o, 3, :, :, a], rows_in.at[o, 2, :, :, a], ups),
            (rows_in.at[o, 1, :, :, b], rows_in.at[o, 2, :, :, b], downs),
        )[k]
        return remote(src, dst, fwd_s.at[o * 4 + k], fwd_r.at[o * 4 + k], to)

    def send_sum(o, k):
        src, to = (
            (partials.at[o, 1, :, :, a], ups),
            (partials.at[o, 3, :, :, b], downs),
            (partials.at[o, 2, :, :, a], downs),
            (partials.at[o, 2, :, :, b], ups),
        )[k]
        return remote(src, arrived.at[o, k], sum_s.at[o * 4 + k], sum_r.at[o * 4 + k], to)

    def back_refs(kind, o, dx, n):
        v, s = (4 - o) % 4, (4 - dx) % 4
        src, dst = pl.ds(3 * dx, n), pl.ds(3 * s, n)
        if kind == 0:
            return partials.at[o, 0, src], returned.at[v, dst]
        if kind == 1:
            return partials.at[o, 3, src, :, a], returned_side.at[0, v, dst]
        return partials.at[o, 1, src, :, b], returned_side.at[1, v, dst]

    def send_back(kind, o, dx):
        src, dst = back_refs(kind, o, dx, 3)
        k = ((4 - o) % 4) * 3 + kind
        return remote(src, dst, back_s.at[k], back_r.at[k], owner(o, dx))

    def all_back(kind, v):
        if v:
            refs = back_refs(kind, (4 - v) % 4, 0, 12)
        else:
            part = pl.ds(3, 9)
            refs = (
                (partials.at[0, 0, part], returned.at[0, part])
                if kind == 0
                else (partials.at[0, 3, part, :, a], returned_side.at[0, 0, part])
                if kind == 1
                else (partials.at[0, 1, part, :, b], returned_side.at[1, 0, part])
            )
        k = v * 3 + kind
        return remote(*refs, back_s.at[k], back_r.at[k], owner(0, 1))

    def pick(k, dz, mine, theirs):
        mark = place[k, dz * group : (dz + 1) * group, :]
        got = jnp.dot(mark[:, 0:tok], mine, preferred_element_type=jnp.float32)
        got += jnp.dot(mark[:, tok:], theirs, preferred_element_type=jnp.float32)
        return got.astype(jnp.bfloat16).reshape(group // 8, 8, half)

    def place_own(o):
        dz = (4 - o) % 4

        for cols in (a, b):
            outgoing[dz, :, :, cols] = pick(0, dz, tokens[:, cols], partner_tokens[:, cols])

        for dx in (2, 1, 3, 0):
            if dz or dx:
                send_zx(0, dz, dx).start()
            else:
                rows_in[0, 0, 0:3] = outgoing[0, 0:3]

    def place_side(o):
        dz = (4 - o) % 4

        outgoing_side[0, dz] = pick(1, dz, below[0], below[1])
        outgoing_side[1, dz] = pick(2, dz, above[0], above[1])

        for dx in (2, 1, 3, 0):
            if dz or dx:
                send_zx(1, dz, dx).start()
                send_zx(2, dz, dx).start()
            else:
                rows_in[0, 3, 0:3, :, 0:half] = outgoing_side[0, 0, 0:3]
                rows_in[0, 1, 0:3, :, half:] = outgoing_side[1, 0, 0:3]

    def forward_own(o):
        all_zx(0, o).wait_recv()
        forward(o, 0).start()
        forward(o, 1).start()

    def forward_side(o):
        all_zx(1, o).wait_recv()
        forward(o, 2).start()
        all_zx(2, o).wait_recv()
        forward(o, 3).start()

    def compute(o, middle):
        for k in range(4):
            forward(o, k).wait_recv()
        for k in range(4):
            lhs[k * group : (k + 1) * group, :] = rows_in[o, k].reshape(group, features)

        @pl.loop(0, hidden.shape[1] // 256)
        def _(n):
            cols = pl.ds(pl.multiple_of(n * 256, 256), 256)
            g = jnp.dot(lhs[...], gate[:, cols], preferred_element_type=jnp.float32)
            u = jnp.dot(lhs[...], up[:, cols], preferred_element_type=jnp.float32)
            hidden[:, cols] = (g / (1.0 + jnp.exp(-g)) * u).astype(jnp.bfloat16)

        if middle is not None:
            if middle == ORDER[2]:
                forward_own(ORDER[3])
            forward_side(middle)

        for side in (0, 1):

            @pl.loop(side * half // 256, (side + 1) * half // 256)
            def _(n):
                cols = pl.ds(pl.multiple_of(n * 256, 256), 256)
                p = jnp.dot(hidden[...], down[:, cols], preferred_element_type=jnp.float32)
                partials[o, :, :, :, cols] = p.astype(jnp.bfloat16).reshape(4, group // 8, 8, 256)

            send_sum(o, 2 + side).start()
            send_sum(o, side).start()

    def added(o, k, part, cols, addends):
        total = partials[o, k, part, :, cols].astype(jnp.float32)
        for addend in addends:
            total += addend[part].astype(jnp.float32)
        return total.astype(jnp.bfloat16)

    def finish(o):
        for which in range(4):
            send_sum(o, which).wait_recv()
        for dx in (2, 1, 3, 0):
            part = pl.ds(3 * dx, 3)
            partials[o, 3, part, :, a] = added(o, 3, part, a, [arrived.at[o, 2]])
            partials[o, 1, part, :, b] = added(o, 1, part, b, [arrived.at[o, 3]])
            partials[o, 0, part, :, a] = added(o, 0, part, a, [arrived.at[o, 0]])
            partials[o, 0, part, :, b] = added(o, 0, part, b, [arrived.at[o, 1]])
            if o or dx:
                for kind in (1, 2, 0):
                    send_back(kind, o, dx).start()
            else:
                returned[0, 0:3] = partials[0, 0, 0:3]
                returned_side[0, 0, 0:3] = partials[0, 3, 0:3, :, 0:half]
                returned_side[1, 0, 0:3] = partials[0, 1, 0:3, :, half:]

    last = ORDER[3]
    unused = (4 - last) % 4
    pass_down = remote(partials.at[last, 3, :, :, a], passed.at[0], pass_s.at[0], pass_r.at[0], downs)
    pass_up = remote(partials.at[last, 1, :, :, b], passed.at[1], pass_s.at[1], pass_r.at[1], ups)

    def pass_sums():
        everything = pl.ds(0, group // 8)
        send_sum(last, 2).wait_recv()
        partials[last, 3, :, :, a] = added(last, 3, everything, a, [arrived.at[last, 2]])
        pass_down.start()
        send_sum(last, 3).wait_recv()
        partials[last, 1, :, :, b] = added(last, 1, everything, b, [arrived.at[last, 3]])
        pass_up.start()

    def finish_last():
        send_sum(last, 0).wait_recv()
        send_sum(last, 1).wait_recv()
        pass_down.wait_recv()
        pass_up.wait_recv()
        for dx in (2, 1, 3, 0):
            part = pl.ds(3 * dx, 3)
            partials[last, 0, part, :, a] = added(last, 0, part, a, [arrived.at[last, 0], passed.at[0]])
            partials[last, 0, part, :, b] = added(last, 0, part, b, [arrived.at[last, 1], passed.at[1]])
            send_back(0, last, dx).start()

    place_own(ORDER[0])
    place_own(ORDER[1])
    for i, (k, c) in enumerate(((1, 0), (1, 1), (2, 0), (2, 1))):
        give_codes[i + 1].wait_recv()
        place[k, :, c * tok : (c + 1) * tok] = marks(other_codes[i + 1, 0:1, :])
    forward_own(ORDER[0])
    give_up.wait_recv()
    swap_below = remote(below.at[0], below.at[1], pair_s.at[2], pair_r.at[2], partner)
    swap_below.start()
    give_down.wait_recv()
    swap_above = remote(above.at[0], above.at[1], pair_s.at[3], pair_r.at[3], partner)
    swap_above.start()
    place_own(ORDER[2])
    swap_below.wait_recv()
    swap_above.wait_recv()
    place_side(ORDER[0])
    place_side(ORDER[1])
    forward_own(ORDER[1])
    place_own(ORDER[3])
    forward_side(ORDER[0])
    place_side(ORDER[2])
    place_side(ORDER[3])
    for w in weights:
        w.wait()
    for i, o in enumerate(ORDER):
        if i == 0:
            forward_own(ORDER[2])
            forward_side(ORDER[1])
        compute(o, ORDER[i + 2] if i + 2 < 4 else None)
        if i >= 2:
            finish(ORDER[i - 2])
    finish(ORDER[2])
    pass_sums()

    slot_lane = lax.broadcasted_iota(jnp.int32, (tok, slots), 1)

    def picks(code_row):
        code = jnp.broadcast_to(code_row, (tok, tok)).T[:, 0:1].astype(jnp.int32)
        return jnp.where(slot_lane == code - shift, 1.0, 0.0).astype(jnp.bfloat16)

    def picked(code_row, source):
        return jnp.dot(picks(code_row), source, preferred_element_type=jnp.float32)

    def picked_last(code_row, source):
        return jnp.dot(
            picks(code_row)[:, unused * group : (unused + 1) * group], source, preferred_element_type=jnp.float32
        )

    for o in ORDER[:3]:
        all_back(1, (4 - o) % 4).wait_recv()
        all_back(2, (4 - o) % 4).wait_recv()
    returned_side[:, unused] = jnp.zeros((2, group // 8, 8, half), jnp.bfloat16)
    for v in range(4):
        rows = slice(v * group, (v + 1) * group)
        lhs[rows, 0:half] = returned_side[0, v].reshape(group, half)
        lhs[rows, half:] = returned_side[1, v].reshape(group, half)
    side_out[0] = picked(other_codes[2, 0:1, :], lhs[:, 0:half]).astype(jnp.bfloat16)
    swap_side_a = remote(side_out.at[0], side_in.at[0], pair_s.at[4], pair_r.at[4], partner)
    swap_side_a.start()
    side_out[1] = picked(other_codes[4, 0:1, :], lhs[:, half:]).astype(jnp.bfloat16)
    swap_side_b = remote(side_out.at[1], side_in.at[1], pair_s.at[5], pair_r.at[5], partner)
    swap_side_b.start()
    mine_a = picked(other_codes[1, 0:1, :], lhs[:, 0:half])
    swap_side_a.wait_recv()
    sides[0] = (mine_a + side_in[0].astype(jnp.float32)).astype(jnp.bfloat16)
    home_down = remote(sides.at[0], home.at[0], home_s.at[0], home_r.at[0], downs)
    home_down.start()
    mine_b = picked(other_codes[3, 0:1, :], lhs[:, half:])
    swap_side_b.wait_recv()
    sides[1] = (mine_b + side_in[1].astype(jnp.float32)).astype(jnp.bfloat16)
    home_up = remote(sides.at[1], home.at[1], home_s.at[1], home_r.at[1], ups)
    home_up.start()
    for o in ORDER[:3]:
        all_back(0, (4 - o) % 4).wait_recv()
    for v in range(4):
        rows = slice(v * group, (v + 1) * group)
        lhs[rows, :] = jnp.zeros((group, features), lhs.dtype) if v == unused else returned[v].reshape(group, features)
    theirs = picked(other_codes[0, 0:1, :], lhs[...])
    mine = picked(codes[0:1, :], lhs[...])
    finish_last()
    all_back(0, unused).wait_recv()
    lhs[0:group, :] = returned[unused].reshape(group, features)
    theirs += picked_last(other_codes[0, 0:1, :], lhs[0:group, :])
    cross_out[...] = theirs.astype(jnp.bfloat16)
    swap_back = remote(cross_out, cross_in, pair_s.at[1], pair_r.at[1], partner)
    swap_back.start()
    mine += picked_last(codes[0:1, :], lhs[0:group, :])
    score = jnp.broadcast_to(scores[...], (tok, tok)).T[:, 0:1]
    swap_back.wait_recv()
    home_down.wait_recv()
    out[:, 0:half] = (
        score * (mine[:, 0:half] + cross_in[:, 0:half].astype(jnp.float32) + home[0].astype(jnp.float32))
    ).astype(jnp.bfloat16)
    home_up.wait_recv()
    out[:, half:] = (
        score * (mine[:, half:] + cross_in[:, half:].astype(jnp.float32) + home[1].astype(jnp.float32))
    ).astype(jnp.bfloat16)

    for c in (
        swap_tokens,
        give_up,
        give_down,
        swap_below,
        swap_above,
        swap_side_a,
        swap_side_b,
        home_down,
        home_up,
        swap_back,
        pass_down,
        pass_up,
        *give_codes,
    ):
        c.wait_send()
    for o in range(4):
        for kind in range(3):
            all_zx(kind, o).wait_send()
            if kind == 0 or o != unused:
                all_back(kind, o).wait_send()
        for k in range(4):
            forward(o, k).wait_send()
            send_sum(o, k).wait_send()


def local(tokens, routes, scores, gate_weight, up_weight, down_weight):
    tok, features = tokens.shape
    hid = gate_weight.shape[2]
    half = features // 2
    slots = 32 * CAP
    group = slots // 4
    g8 = group // 8
    bf = jnp.bfloat16
    vmem = pl.BlockSpec(memory_space=pltpu.VMEM)
    hbm = pl.BlockSpec(memory_space=pl.ANY)
    sizes = (
        (features, hid),
        (features, hid),
        (hid, features),
        None,
        None,
        (tok, features),
        (2, tok, half),
        (2, tok, half),
        (3, slots, 2 * tok),
        (4, g8, 8, features),
        (2, 4, g8, 8, half),
        (4, 4, g8, 8, features),
        (slots, features),
        (slots, hid),
        (4, 4, g8, 8, features),
        (4, 4, g8, 8, half),
        (4, g8, 8, features),
        (2, 4, g8, 8, half),
        (tok, features),
        (tok, features),
        (2, tok, half),
        (2, tok, half),
        (2, tok, half),
        (2, tok, half),
        (2, g8, 8, half),
    )
    scratch = [pltpu.VMEM(s, bf) if s else None for s in sizes]
    scratch[3] = pltpu.VMEM((8, tok), jnp.float32)
    scratch[4] = pltpu.VMEM((5, 8, tok), jnp.float32)
    counts = (3, 6, 6, 5, 5, 2, 2, 12, 12, 16, 16, 16, 16, 12, 12, 2, 2, 2, 2)
    return pl.pallas_call(
        layer,
        out_shape=jax.ShapeDtypeStruct((tok, features), bf),
        in_specs=[vmem] * 3 + [hbm] * 3,
        out_specs=vmem,
        scratch_shapes=scratch + [pltpu.SemaphoreType.DMA((n,)) for n in counts],
        compiler_params=pltpu.CompilerParams(
            collective_id=0, has_side_effects=True, vmem_limit_bytes=62 * 1024 * 1024
        ),
    )(
        tokens,
        routes.reshape(1, tok),
        scores.reshape(1, tok),
        gate_weight[0],
        up_weight[0],
        down_weight[0],
    )


def solution(mesh):
    in_specs = (
        P(("expert", "etp"), None),
        P(("expert", "etp"), None),
        P(("expert", "etp")),
        P("expert", None, "etp"),
        P("expert", None, "etp"),
        P("expert", "etp", None),
    )
    out_specs = P(("expert", "etp"), None)
    return jax.shard_map(local, mesh=mesh, in_specs=in_specs, out_specs=out_specs, check_vma=False)
```
